32 devices in a mesh: group: 2 (over y), seq: 4 (over z), blk: 2 (over x), tp: 2 (over core).
Axes of the slice: x: 2, y: 2, z: 4, core: 2. Of those that a mesh axis runs over, the one named last changes fastest.
Arguments:
- tokens: bfloat16 [2048, 3072], P(('group', 'blk'), ('seq', 'tp')), parts along dimension 0, may hold values from -64 to 64
- timestep: int32 [2], P('group'), parts along dimension 0, may hold values from 25 to 49
- padded_heads: int32 [2], P('group'), parts along dimension 0, may hold values from 1 to 3
- modulation: float32 [50, 3, 3072], replicated, may hold values from -3 to 3
- qkv_weight: bfloat16 [3, 3072, 1024], P(None, 'blk', ('seq', 'tp')), may hold values from -1 to 1
- out_weight: bfloat16 [1024, 3072], P(('seq', 'tp'), 'blk'), may hold values from -0.5 to 0.5
Outputs:
- update: bfloat16 [2048, 3072], P(('group', 'blk'), ('seq', 'tp')), parts along dimension 0
The draws below stay inside these ranges and needn't reach their ends.
There are 2 independent parts, one for each index of `group`. The reference program is written for one: setup_inputs(seed, part) draws one part's arguments, and reference() takes and returns one part's arrays. A program takes and returns all parts, laid end to end along the dimension named above; an argument that names none is the same for every part. Nothing has to cross between parts.
All inputs are finite; a program needn't handle non-finite values.
Results may differ from the reference program's by a relative error of at most 0.023.
Values may be sent and summed in bfloat16 or wider, within the bound.
A program may use at most 64 MiB of HBM per device.

```python
import math
import jax
import jax.numpy as jnp
from jax import lax

D = 3072
E = 128
STEPS = 50
HEADS = 8
TOKENS = 1024


def draw_tokens(key, part):
    noise_key = jax.random.fold_in(key, 0)
    column_key = jax.random.fold_in(key, 1)
    mean_key = jax.random.fold_in(key, 3)
    column = jnp.arange(D, dtype=jnp.float32) / max(D - 1, 1)
    rising = jnp.exp(math.log(3.0) * column) * jax.random.uniform(column_key, (D,), jnp.float32, 0.7, 1.4)
    noise = jax.random.normal(noise_key, (TOKENS, D), jnp.float32)
    offset = 0.5 * jax.random.normal(mean_key, (TOKENS, 1), jnp.float32)
    result = (noise + offset) * rising
    return jnp.clip(result, -64.0, 64.0).astype(jnp.bfloat16)


def draw_qkv_weight(key, part):
    noise_key = jax.random.fold_in(key, 0)
    sigma = 1.2 / math.sqrt(D)
    result = jax.random.normal(noise_key, (3, D, HEADS * E), jnp.float32) * sigma
    return jnp.clip(result, -1.0, 1.0).astype(jnp.bfloat16)


def shard_levels(rng, shape, cuts, low, high):
    factor_of = 1.0
    for dim, shards_of in cuts:
        draws = jax.random.uniform(jax.random.fold_in(jax.random.fold_in(rng, 6), dim), (shards_of,), jnp.float32, low / len(cuts), high / len(cuts))
        factor_of = factor_of * jnp.repeat(jnp.exp(draws), shape[dim] // shards_of).reshape((-1,) + (1,) * (len(shape) - 1 - dim))
    return factor_of


def centred(own_key, extent, deviation, most, cuts=(), kind=jnp.bfloat16):
    values = jax.random.normal(own_key, extent, jnp.float32) * deviation
    if len(cuts) > 0:
        values = shard_levels(own_key, extent, cuts, -0.22, 0.18) * values
    return jnp.clip(values, min=-most, max=most).astype(kind)


def setup_inputs(seed: int = 0, part: int = 0) -> dict:
    seeds = jax.random.split(jax.random.key(seed), 7)
    part_splits = jax.random.split(jax.random.fold_in(seeds[6], part), 7)
    return {
        "tokens": draw_tokens(jax.random.fold_in(jax.random.fold_in(seeds[6], part), 71), part),
        "timestep": jax.random.randint(part_splits[1], (1,), STEPS // 2, STEPS).astype(jnp.int32),
        "padded_heads": jax.random.randint(part_splits[2], (1,), HEADS // 8, HEADS * 3 // 8 + 1).astype(jnp.int32),
        "modulation": centred(seeds[3], (STEPS, 3, D), 0.5, 3.0, (), jnp.float32),
        "qkv_weight": draw_qkv_weight(jax.random.fold_in(seeds[6], 71), part),
        "out_weight": centred(seeds[5], (HEADS * E, D), E ** -0.5, 0.5, ((0, 8), (1, 2))),
    }


epsilon = 1e-06

def reference(tokens, timestep, padded_heads, modulation, qkv_weight, out_weight):
    table_row = lax.dynamic_index_in_dim(modulation, timestep[0], 0, keepdims=False)
    values = tokens.astype(jnp.float32)
    average = lax.optimization_barrier(jnp.mean(values, axis=1, keepdims=True))
    centered = values - average
    spread = lax.optimization_barrier(jnp.mean(centered * centered, axis=1, keepdims=True))
    normed = centered * lax.rsqrt(spread + epsilon)
    modulated = (normed * (1.0 + table_row[1]) + table_row[0]).astype(jnp.bfloat16)
    queries = jnp.dot(modulated, qkv_weight[0], preferred_element_type=jnp.float32).astype(jnp.bfloat16)
    keys_all = jnp.dot(modulated, qkv_weight[1], preferred_element_type=jnp.float32).astype(jnp.bfloat16)
    values_all = jnp.dot(modulated, qkv_weight[2], preferred_element_type=jnp.float32).astype(jnp.bfloat16)
    live_heads = HEADS - padded_heads[0]
    factor = 1.0 / math.sqrt(E)

    def one_head(running, head_index):
        query_head = lax.dynamic_slice_in_dim(queries, head_index * E, E, 1)
        key_head = lax.dynamic_slice_in_dim(keys_all, head_index * E, E, 1)
        value_head = lax.dynamic_slice_in_dim(values_all, head_index * E, E, 1)
        scores = lax.dot_general(query_head, key_head, (((1,), (1,)), ((), ())), preferred_element_type=jnp.float32) * factor
        largest = lax.optimization_barrier(jnp.max(scores, axis=1, keepdims=True))
        weights = jnp.exp(scores - largest)
        totals = lax.optimization_barrier(jnp.sum(weights, axis=1, keepdims=True))
        attended = jnp.dot(weights.astype(jnp.bfloat16), value_head, preferred_element_type=jnp.float32) / totals
        masked = jnp.where(head_index < live_heads, attended, 0.0).astype(jnp.bfloat16)
        out_rows = lax.dynamic_slice_in_dim(out_weight, head_index * E, E, 0)
        head_term = jnp.dot(masked, out_rows, preferred_element_type=jnp.float32).astype(jnp.bfloat16)
        head_term = lax.optimization_barrier(head_term).astype(jnp.float32)
        return (running + head_term, None)
    summed, ignored = lax.scan(one_head, jnp.zeros((TOKENS, D), jnp.float32), jnp.arange(HEADS, dtype=jnp.int32))
    return (table_row[2] * summed).astype(jnp.bfloat16)
```

```python
import functools
import math

import jax
import jax.numpy as jnp
from jax import lax
from jax.experimental import pallas as pl
from jax.experimental.pallas import tpu as pltpu
from jax.sharding import PartitionSpec as P

epsilon = 1e-06
neg_large = -1e30


def collect(own_part):
    gathered = lax.all_gather(own_part, ("seq", "tp"), axis=1, tiled=True)
    return gathered


def attend_block(running, queries, key_block, value_block, factor):
    largest, totals, weighted = running
    scores = (
        lax.dot_general(
            queries, key_block, (((1,), (1,)), ((), ())), preferred_element_type=jnp.float32
        )
        * factor
    )
    new_max = jnp.maximum(largest, jnp.max(scores, axis=1))
    rescale = jnp.exp(largest - new_max)
    weights = jnp.exp(scores - new_max[:, None])
    totals = totals * rescale + jnp.sum(weights, axis=1)
    weighted = weighted * rescale[:, None] + jnp.dot(
        weights.astype(jnp.bfloat16), value_block, preferred_element_type=jnp.float32
    )
    return (new_max, totals, weighted)


def body(tokens, timestep, padded_heads, modulation, qkv_weight, out_weight):
    slices = lax.axis_size(("seq", "tp"))
    own_index = lax.axis_index(("seq", "tp"))
    model_width = modulation.shape[2]
    own_width = model_width // slices
    token_rows = tokens.shape[0]
    head_size = out_weight.shape[0]
    table_row = lax.dynamic_index_in_dim(modulation, timestep[0], 0, keepdims=False)
    own_entry = lax.dynamic_slice_in_dim(table_row, own_index * own_width, own_width, 1)
    gathered = collect(tokens).astype(jnp.float32)
    average = jnp.mean(gathered, axis=1, keepdims=True)
    centered = gathered - average
    spread = jnp.mean(centered * centered, axis=1, keepdims=True)
    normed = centered * lax.rsqrt(spread + epsilon)
    modulated = (normed * (1.0 + table_row[1]) + table_row[0]).astype(jnp.bfloat16)
    projected = jnp.einsum(
        "td,kde->kte",
        modulated,
        lax.all_gather(qkv_weight, "blk", axis=1, tiled=True),
        preferred_element_type=jnp.float32,
    ).astype(jnp.bfloat16)
    queries = projected[0]
    factor = 1.0 / math.sqrt(head_size)
    initial = (
        jnp.full((token_rows,), neg_large, jnp.float32),
        jnp.zeros((token_rows,), jnp.float32),
        jnp.zeros((token_rows, head_size), jnp.float32),
    )
    key_piece = lax.all_gather(projected[1], "blk", axis=0, tiled=True)
    value_piece = lax.all_gather(projected[2], "blk", axis=0, tiled=True)
    length = key_piece.shape[0]

    def one_block(counter, inner_state):
        key_block = lax.dynamic_slice_in_dim(key_piece, counter * 512, 512, 0)
        value_block = lax.dynamic_slice_in_dim(value_piece, counter * 512, 512, 0)
        return attend_block(inner_state, queries, key_block, value_block, factor)

    largest, exp_totals, weighted = lax.fori_loop(0, length // 512, one_block, initial)
    attended = weighted / exp_totals[:, None]
    live_heads = slices - padded_heads[0]
    masked = jnp.where(own_index < live_heads, attended, 0.0).astype(jnp.bfloat16)
    head_term = jnp.dot(
        masked,
        lax.all_gather(out_weight, "blk", axis=1, tiled=True),
        preferred_element_type=jnp.float32,
    )
    summed = lax.psum_scatter(
        head_term.astype(jnp.bfloat16), ("seq", "tp"), scatter_dimension=1, tiled=True
    ).astype(jnp.float32)
    return (own_entry[2] * summed).astype(jnp.bfloat16)


MESH = pl.DeviceIdType.MESH
bf16, f32 = jnp.bfloat16, jnp.float32


def fused_kernel(
    dims,
    tokens_ref,
    table_ref,
    qkv_ref,
    out_weight_ref,
    out_ref,
    tok,
    mod,
    wts,
    query,
    kv,
    att,
    wout,
    local_sem,
    tok_send,
    tok_recv,
    w_send,
    w_recv,
    kv_send,
    kv_recv,
    att_send,
    att_recv,
    o_send,
    o_recv,
    f_send,
    f_recv,
):
    S, chunks, pieces = dims
    rows, width = tokens_ref.shape
    kinds, half, size = qkv_ref.shape
    slices = 2 * S
    g, z = lax.axis_index("group"), lax.axis_index("seq")
    x, c = lax.axis_index("blk"), lax.axis_index("tp")
    own = z * 2 + c
    R = rows // chunks
    A = rows // pieces
    part = half // 2
    hpart = size // 2

    up, down = (g, z + 1, x, c), (g, z - 1, x, c)
    mate = (g, z, x, 1 - c)
    over = (g, z, 1 - x, c)
    twin = (1 - g, z, x, c)

    def remote(src, dst, s_sem, r_sem, where):
        return pltpu.make_async_remote_copy(
            src_ref=src,
            dst_ref=dst,
            send_sem=s_sem,
            recv_sem=r_sem,
            device_id=where,
            device_id_type=MESH,
        )

    def lanes(index, extent):
        return pl.ds(pl.multiple_of(index * extent, 128), extent)

    def tok_at(s, r):
        return tok.at[pl.ds(r * R, R), lanes(s, width)]

    def att_at(s, r):
        return att.at[pl.ds(r * A, A), lanes(s, size)]

    def tok_copy(way, s, r, where, src=None):
        there = tok_at(s, r)
        return remote(there if src is None else src, there, tok_send.at[way, s, r], tok_recv.at[s, r], where)

    def att_copy(way, s, r, where, src=None):
        there = att_at(s, r)
        return remote(there, there, att_send.at[way, s, r], att_recv.at[s, r], where)

    def send_own(make, r, src=None):
        @pl.when(z < S - 1)
        def _():
            make(0, own, r, up, src).start()

        @pl.when(z > 0)
        def _():
            make(1, own, r, down, src).start()

        make(2, own, r, mate, src).start()

    def relay(make, d, r):
        @pl.when(z - d >= 0)
        def _():
            s = (z - d) * 2 + c
            make(0, s, r, up).wait_recv()

            @pl.when(z < S - 1)
            def _():
                make(0, s, r, up).start()

            make(2, s, r, mate).start()

        @pl.when(z + d < S)
        def _():
            s = (z + d) * 2 + c
            make(1, s, r, down).wait_recv()

            @pl.when(z > 0)
            def _():
                make(1, s, r, down).start()

            make(2, s, r, mate).start()

    def wait_mates(make, r):
        for other in range(S):
            make(2, other * 2 + 1 - c, r, mate).wait_recv()

    def drain(make, count):
        for r in range(count):
            for other in range(S):
                s = other * 2 + c

                @pl.when((z < S - 1) & (other <= z))
                def _():
                    make(0, s, r, up).wait_send()

                @pl.when((z > 0) & (other >= z))
                def _():
                    make(1, s, r, down).wait_send()

                make(2, s, r, mate).wait_send()

    def w_at(block, p, i):
        first = pl.multiple_of(block * half + p * part, 16)
        return wts.at[pl.ds(first, part), pl.ds(i * size, size)]

    def w_over(i):
        src = qkv_ref.at[i, pl.ds(pl.multiple_of(g * part, 16), part)]
        return remote(src, w_at(x, g, i), w_send.at[0, i], w_recv.at[0, i], over)

    def w_over_in(i):
        there = w_at(1 - x, g, i)
        return remote(there, there, w_send.at[0, i], w_recv.at[0, i], over)

    def w_twin(i):
        there = w_at(1 - x, g, i)
        return remote(there, there, w_send.at[1, i], w_recv.at[1, i], twin)

    def w_twin_in(i):
        there = w_at(1 - x, 1 - g, i)
        return remote(there, there, w_send.at[1, i], w_recv.at[1, i], twin)

    def o_at(head, p):
        return wout.at[head, pl.ds(pl.multiple_of(p * hpart, 16), hpart)]

    def o_src(j):
        return out_weight_ref.at[pl.ds(pl.multiple_of(g * hpart, 16), hpart), pl.ds(j * width, width)]

    per_blk = slices // 2
    home = own // per_blk == x

    def o_copy(j):
        s = x * per_blk + j
        return remote(o_src(j), o_at(own, g), o_send.at[j], o_recv.at[own], (g, s // 2, x, s % 2))

    def o_local(j):
        return pltpu.make_async_copy(o_src(j), o_at(own, g), local_sem.at[5])

    def o_in(head):
        return remote(o_at(head, g), o_at(head, g), o_send.at[0], o_recv.at[head], mate)

    def o_all(p):
        return wout.at[:, pl.ds(pl.multiple_of(p * hpart, 16), hpart)]

    def f_over():
        return remote(o_all(g), o_all(g), f_send.at[0], f_recv.at[0], over)

    def f_twin():
        return remote(o_all(g), o_all(g), f_send.at[1], f_recv.at[1], twin)

    def f_twin_in():
        return remote(o_all(1 - g), o_all(1 - g), f_send.at[1], f_recv.at[1], twin)

    def kv_at(block, r):
        return kv.at[block, :, pl.ds(r * R, R)]

    def kv_copy(block, r):
        return remote(kv_at(block, r), kv_at(block, r), kv_send.at[r], kv_recv.at[r], over)

    barrier = pltpu.get_barrier_semaphore()
    for step in range(1, slices):
        s = lax.rem(own + step, slices)
        pl.semaphore_signal(barrier, inc=1, device_id=(g, s // 2, x, s % 2), device_id_type=MESH)
    for where in (over, twin):
        pl.semaphore_signal(barrier, inc=1, device_id=where, device_id_type=MESH)
    locals_ = [pltpu.make_async_copy(tokens_ref, tok.at[:, lanes(own, width)], local_sem.at[0])]
    for i in range(kinds):
        there = wts.at[pl.ds(pl.multiple_of(x * half, 16), half), pl.ds(i * size, size)]
        locals_.append(pltpu.make_async_copy(qkv_ref.at[i], there, local_sem.at[1 + i]))
    for copy in locals_:
        copy.start()
    pl.semaphore_wait(barrier, slices + 1)

    for r in range(chunks):
        send_own(tok_copy, r, tokens_ref.at[pl.ds(r * R, R)])
    for i in range(kinds):
        w_over(i).start()
    for copy in locals_:
        copy.wait()

    def normalise(r):
        group_rows = 16

        def one(i, carry):
            at = pl.multiple_of(r * R + i * group_rows, group_rows)
            values = tok[pl.ds(at, group_rows), :].astype(f32)
            centered = values - jnp.mean(values, axis=1, keepdims=True)
            spread = jnp.mean(centered * centered, axis=1, keepdims=True)
            normed = centered * lax.rsqrt(spread + epsilon)
            to = pl.multiple_of(i * group_rows, group_rows)
            mod[pl.ds(to, group_rows), :] = (normed * (1.0 + table_ref[1:2, :]) + table_ref[0:1, :]).astype(bf16)
            return carry

        lax.fori_loop(0, R // group_rows, one, 0)

    def compute(r):
        wait_mates(tok_copy, r)
        normalise(r)
        if r == 0:
            for i in range(kinds):
                w_twin_in(i).wait_recv()
        projected = jnp.dot(mod[...], wts[...], preferred_element_type=f32).astype(bf16)
        query[pl.ds(r * R, R), :] = projected[:, :size]
        kv[x, 0, pl.ds(r * R, R), :] = projected[:, size : 2 * size]
        kv[x, 1, pl.ds(r * R, R), :] = projected[:, 2 * size :]
        kv_copy(x, r).start()

    forwarded = 0
    for d in range(1, S):
        last = d == S - 1
        for r in range(chunks):
            relay(tok_copy, d, r)
            if r % 2 == 1 and forwarded < kinds:
                w_over_in(forwarded).wait_recv()
                w_twin(forwarded).start()
                forwarded += 1
            if last and r > 0:
                compute(r - 1)
        if d == S - 2:
            for j in range(per_blk):
                s = x * per_blk + j

                @pl.when(s == own)
                def _():
                    o_local(j).start()

                @pl.when(s != own)
                def _():
                    o_copy(j).start()

    compute(chunks - 1)
    for j in range(per_blk):
        s = x * per_blk + j

        @pl.when(s == own)
        def _():
            o_local(j).wait()

    for r in range(chunks):
        kv_copy(1 - x, r).wait_recv()

    factor = 1.0 / math.sqrt(size)
    contract = (((1,), (1,)), ((), ()))

    def attend(r):
        q = query[pl.ds(r * A, A), :]
        scores = [
            lax.dot_general(q, kv[b, 0], contract, preferred_element_type=f32) * factor for b in range(2)
        ]
        largest = jnp.maximum(
            jnp.max(scores[0], axis=1, keepdims=True), jnp.max(scores[1], axis=1, keepdims=True)
        )
        total, weighted = 0.0, 0.0
        for b in range(2):
            weights = jnp.exp(scores[b] - largest)
            total = total + jnp.sum(weights, axis=1, keepdims=True)
            weighted = weighted + jnp.dot(weights.astype(bf16), kv[b, 1], preferred_element_type=f32)
        attended = weighted / total
        masked = jnp.where(table_ref[3:4, :size] > 0.0, attended, 0.0).astype(bf16)
        att[pl.ds(r * A, A), lanes(own, size)] = masked
        send_own(att_copy, r)

    for r in range(pieces):
        attend(r)

    @pl.when(home)
    def _():
        for step in range(1, slices):
            o_in(lax.rem(own + step, slices)).wait_recv()
        f_over().start()
        f_twin().start()

    for d in range(1, S):
        for r in range(pieces):
            relay(att_copy, d, r)
        if d == 1:

            @pl.when(jnp.logical_not(home))
            def _():
                f_over().wait_recv()
                f_twin().start()

    f_twin_in().wait_recv()
    gate = table_ref[2:3, lanes(own, width)]
    weight = wout[...].reshape(slices * size, width)
    for r in range(pieces):
        wait_mates(att_copy, r)
        summed = jnp.dot(att[pl.ds(r * A, A), :], weight, preferred_element_type=f32)
        out_ref[pl.ds(r * A, A), :] = (gate * summed).astype(bf16)

    drain(tok_copy, chunks)
    drain(att_copy, pieces)
    for i in range(kinds):
        w_over(i).wait_send()
        w_twin(i).wait_send()
    for r in range(chunks):
        kv_copy(x, r).wait_send()
    for j in range(per_blk):
        s = x * per_blk + j

        @pl.when(s != own)
        def _():
            o_copy(j).wait_send()

    f_twin().wait_send()

    @pl.when(home)
    def _():
        f_over().wait_send()


def fused_body(S, tokens, timestep, padded_heads, modulation, qkv_weight, out_weight):
    slices = 2 * S
    rows, width = tokens.shape
    kinds, half, size = qkv_weight.shape
    model_width = modulation.shape[2]
    chunks, pieces = 4, 2
    table_row = lax.dynamic_index_in_dim(modulation, timestep[0], 0, keepdims=False)
    live = lax.axis_index(("seq", "tp")) < slices - padded_heads[0]
    table = jnp.concatenate([table_row, jnp.full((1, model_width), live.astype(f32))], axis=0)
    anywhere = pl.BlockSpec(memory_space=pl.ANY)
    vmem = pl.BlockSpec(memory_space=pltpu.VMEM)
    dma = pltpu.SemaphoreType.DMA
    return pl.pallas_call(
        functools.partial(fused_kernel, (S, chunks, pieces)),
        out_shape=jax.ShapeDtypeStruct((rows, width), bf16),
        in_specs=[anywhere, vmem, anywhere, anywhere],
        out_specs=vmem,
        scratch_shapes=[
            pltpu.VMEM((rows, model_width), bf16),
            pltpu.VMEM((rows // chunks, model_width), bf16),
            pltpu.VMEM((model_width, kinds * size), bf16),
            pltpu.VMEM((rows, size), bf16),
            pltpu.VMEM((2, 2, rows, size), bf16),
            pltpu.VMEM((rows, slices * size), bf16),
            pltpu.VMEM((slices, size, width), bf16),
            dma((6,)),
            dma((3, slices, chunks)),
            dma((slices, chunks)),
            dma((2, kinds)),
            dma((2, kinds)),
            dma((chunks,)),
            dma((chunks,)),
            dma((3, slices, pieces)),
            dma((slices, pieces)),
            dma((slices // 2,)),
            dma((slices,)),
            dma((2,)),
            dma((2,)),
        ],
        compiler_params=pltpu.CompilerParams(collective_id=0, has_side_effects=True),
    )(tokens, table, qkv_weight, out_weight)


def fits(mesh):
    shape = mesh.shape
    return shape["group"] == 2 and shape["blk"] == 2 and shape["tp"] == 2 and shape["seq"] >= 3


def solution(mesh):
    chosen = functools.partial(fused_body, mesh.shape["seq"]) if fits(mesh) else body
    return jax.shard_map(
        chosen,
        mesh=mesh,
        in_specs=(
            P(("group", "blk"), ("seq", "tp")),
            P("group"),
            P("group"),
            P(),
            P(None, "blk", ("seq", "tp")),
            P(("seq", "tp"), "blk"),
        ),
        out_specs=P(("group", "blk"), ("seq", "tp")),
        check_vma=False,
    )
```

```python
import functools
import math

import jax
import jax.numpy as jnp
from jax import lax
from jax.experimental import pallas as pl
from jax.experimental.pallas import tpu as pltpu
from jax.sharding import PartitionSpec as P

epsilon = 1e-06
neg_large = -1e30


def collect(own_part):
    gathered = lax.all_gather(own_part, ("seq", "tp"), axis=1, tiled=True)
    return gathered


def attend_block(running, queries, key_block, value_block, factor):
    largest, totals, weighted = running
    scores = (
        lax.dot_general(
            queries, key_block, (((1,), (1,)), ((), ())), preferred_element_type=jnp.float32
        )
        * factor
    )
    new_max = jnp.maximum(largest, jnp.max(scores, axis=1))
    rescale = jnp.exp(largest - new_max)
    weights = jnp.exp(scores - new_max[:, None])
    totals = totals * rescale + jnp.sum(weights, axis=1)
    weighted = weighted * rescale[:, None] + jnp.dot(
        weights.astype(jnp.bfloat16), value_block, preferred_element_type=jnp.float32
    )
    return (new_max, totals, weighted)


def body(tokens, timestep, padded_heads, modulation, qkv_weight, out_weight):
    slices = lax.axis_size(("seq", "tp"))
    own_index = lax.axis_index(("seq", "tp"))
    model_width = modulation.shape[2]
    own_width = model_width // slices
    token_rows = tokens.shape[0]
    head_size = out_weight.shape[0]
    table_row = lax.dynamic_index_in_dim(modulation, timestep[0], 0, keepdims=False)
    own_entry = lax.dynamic_slice_in_dim(table_row, own_index * own_width, own_width, 1)
    gathered = collect(tokens).astype(jnp.float32)
    average = jnp.mean(gathered, axis=1, keepdims=True)
    centered = gathered - average
    spread = jnp.mean(centered * centered, axis=1, keepdims=True)
    normed = centered * lax.rsqrt(spread + epsilon)
    modulated = (normed * (1.0 + table_row[1]) + table_row[0]).astype(jnp.bfloat16)
    projected = jnp.einsum(
        "td,kde->kte",
        modulated,
        lax.all_gather(qkv_weight, "blk", axis=1, tiled=True),
        preferred_element_type=jnp.float32,
    ).astype(jnp.bfloat16)
    queries = projected[0]
    factor = 1.0 / math.sqrt(head_size)
    initial = (
        jnp.full((token_rows,), neg_large, jnp.float32),
        jnp.zeros((token_rows,), jnp.float32),
        jnp.zeros((token_rows, head_size), jnp.float32),
    )
    key_piece = lax.all_gather(projected[1], "blk", axis=0, tiled=True)
    value_piece = lax.all_gather(projected[2], "blk", axis=0, tiled=True)
    length = key_piece.shape[0]

    def one_block(counter, inner_state):
        key_block = lax.dynamic_slice_in_dim(key_piece, counter * 512, 512, 0)
        value_block = lax.dynamic_slice_in_dim(value_piece, counter * 512, 512, 0)
        return attend_block(inner_state, queries, key_block, value_block, factor)

    largest, exp_totals, weighted = lax.fori_loop(0, length // 512, one_block, initial)
    attended = weighted / exp_totals[:, None]
    live_heads = slices - padded_heads[0]
    masked = jnp.where(own_index < live_heads, attended, 0.0).astype(jnp.bfloat16)
    head_term = jnp.dot(
        masked,
        lax.all_gather(out_weight, "blk", axis=1, tiled=True),
        preferred_element_type=jnp.float32,
    )
    summed = lax.psum_scatter(
        head_term.astype(jnp.bfloat16), ("seq", "tp"), scatter_dimension=1, tiled=True
    ).astype(jnp.float32)
    return (own_entry[2] * summed).astype(jnp.bfloat16)


MESH = pl.DeviceIdType.MESH
bf16, f32 = jnp.bfloat16, jnp.float32


def fused_kernel(
    dims,
    tokens_ref,
    step_ref,
    padded_ref,
    modulation_ref,
    qkv_ref,
    out_weight_ref,
    out_ref,
    step_smem,
    padded_smem,
    modulation,
    tok,
    mod,
    wts,
    query,
    kv,
    att,
    wout,
    outw,
    table,
    local_sem,
    tok_send,
    tok_recv,
    w_send,
    w_recv,
    kv_send,
    kv_recv,
    att_send,
    att_recv,
    o_send,
    o_recv,
):
    S, chunks, pieces = dims
    rows, width = tokens_ref.shape
    kinds, half, size = qkv_ref.shape
    slices = 2 * S
    g, z = lax.axis_index("group"), lax.axis_index("seq")
    x, c = lax.axis_index("blk"), lax.axis_index("tp")
    own = z * 2 + c
    R = rows // chunks
    A = rows // pieces
    part = half // 2
    hpart = size // 2

    up, down = (g, z + 1, x, c), (g, z - 1, x, c)
    mate = (g, z, x, 1 - c)
    over = (g, z, 1 - x, c)
    twin = (1 - g, z, x, c)

    def remote(src, dst, s_sem, r_sem, where):
        return pltpu.make_async_remote_copy(
            src_ref=src,
            dst_ref=dst,
            send_sem=s_sem,
            recv_sem=r_sem,
            device_id=where,
            device_id_type=MESH,
        )

    def lanes(index, extent):
        return pl.ds(pl.multiple_of(index * extent, 128), extent)

    def tok_at(s, r):
        return tok.at[pl.ds(r * R, R), lanes(s, width)]

    def att_at(s, r):
        return att.at[pl.ds(r * A, A), lanes(s, size)]

    def tok_copy(way, s, r, where, src=None):
        there = tok_at(s, r)
        return remote(there if src is None else src, there, tok_send.at[way, s, r], tok_recv.at[s, r], where)

    def att_copy(way, s, r, where, src=None):
        there = att_at(s, r)
        return remote(there, there, att_send.at[way, s, r], att_recv.at[s, r], where)

    def send_own(make, r, src=None):
        @pl.when(z < S - 1)
        def _():
            make(0, own, r, up, src).start()

        @pl.when(z > 0)
        def _():
            make(1, own, r, down, src).start()

        make(2, own, r, mate, src).start()

    def relay(make, d, r):
        @pl.when(z - d >= 0)
        def _():
            s = (z - d) * 2 + c
            make(0, s, r, up).wait_recv()

            @pl.when(z < S - 1)
            def _():
                make(0, s, r, up).start()

            make(2, s, r, mate).start()

        @pl.when(z + d < S)
        def _():
            s = (z + d) * 2 + c
            make(1, s, r, down).wait_recv()

            @pl.when(z > 0)
            def _():
                make(1, s, r, down).start()

            make(2, s, r, mate).start()

    def wait_mates(make, r):
        for other in range(S):
            make(2, other * 2 + 1 - c, r, mate).wait_recv()

    def drain(make, count):
        for r in range(count):
            for other in range(S):
                s = other * 2 + c

                @pl.when((z < S - 1) & (other <= z))
                def _():
                    make(0, s, r, up).wait_send()

                @pl.when((z > 0) & (other >= z))
                def _():
                    make(1, s, r, down).wait_send()

                make(2, s, r, mate).wait_send()

    def w_at(block, p, i):
        first = pl.multiple_of(block * half + p * part, 16)
        return wts.at[pl.ds(first, part), pl.ds(i * size, size)]

    def w_over(i):
        src = qkv_ref.at[i, pl.ds(pl.multiple_of(g * part, 16), part)]
        return remote(src, w_at(x, g, i), w_send.at[0, i], w_recv.at[0, i], over)

    def w_over_in(i):
        there = w_at(1 - x, g, i)
        return remote(there, there, w_send.at[0, i], w_recv.at[0, i], over)

    def w_twin(i):
        there = w_at(1 - x, g, i)
        return remote(there, there, w_send.at[1, i], w_recv.at[1, i], twin)

    def w_twin_in(i):
        there = w_at(1 - x, 1 - g, i)
        return remote(there, there, w_send.at[1, i], w_recv.at[1, i], twin)

    def o_at(head, p):
        return wout.at[head, pl.ds(pl.multiple_of(p * hpart, 16), hpart)]

    def o_over(block):
        src = out_weight_ref.at[pl.ds(pl.multiple_of(g * hpart, 16), hpart)]
        return remote(src, outw.at[block], o_send.at[0, 0], o_recv.at[0, 0], over)

    per_blk = slices // 2

    def o_src(s):
        return outw.at[s // per_blk, :, lanes(lax.rem(s, per_blk), width)]

    def o_copy(step):
        s = lax.rem(own + step, slices)
        return remote(o_src(s), o_at(own, g), o_send.at[1, step], o_recv.at[1, own], (g, s // 2, x, s % 2))

    def o_in(head):
        return remote(o_at(head, g), o_at(head, g), o_send.at[1, 0], o_recv.at[1, head], mate)

    def o_twin(head, p):
        return remote(o_at(head, p), o_at(head, p), o_send.at[2, head], o_recv.at[2, head], twin)

    def kv_at(block, r):
        return kv.at[block, :, pl.ds(r * R, R)]

    def kv_copy(block, r):
        return remote(kv_at(block, r), kv_at(block, r), kv_send.at[r], kv_recv.at[r], over)

    barrier = pltpu.get_barrier_semaphore()
    for step in range(1, slices):
        s = lax.rem(own + step, slices)
        pl.semaphore_signal(barrier, inc=1, device_id=(g, s // 2, x, s % 2), device_id_type=MESH)
    for where in (over, twin):
        pl.semaphore_signal(barrier, inc=1, device_id=where, device_id_type=MESH)
    locals_ = [
        pltpu.make_async_copy(tokens_ref, tok.at[:, lanes(own, width)], local_sem.at[0]),
        pltpu.make_async_copy(step_ref, step_smem, local_sem.at[6]),
        pltpu.make_async_copy(padded_ref, padded_smem, local_sem.at[7]),
        pltpu.make_async_copy(modulation_ref, modulation, local_sem.at[8]),
        pltpu.make_async_copy(
            out_weight_ref.at[pl.ds(pl.multiple_of(g * hpart, 16), hpart)], outw.at[x], local_sem.at[9]
        ),
    ]
    for i in range(kinds):
        there = wts.at[pl.ds(pl.multiple_of(x * half, 16), half), pl.ds(i * size, size)]
        locals_.append(pltpu.make_async_copy(qkv_ref.at[i], there, local_sem.at[1 + i]))
    for copy in locals_:
        copy.start()
    pl.semaphore_wait(barrier, slices + 1)

    for r in range(chunks):
        send_own(tok_copy, r, tokens_ref.at[pl.ds(r * R, R)])
    for i in range(kinds):
        w_over(i).start()
    o_over(x).start()
    for copy in locals_:
        copy.wait()
    row = pl.ds(step_smem[0], 1)
    table[0:1, :] = 1.0 + modulation[1, row, :]
    table[1:2, :] = modulation[0, row, :]
    table[2:3, :] = modulation[2, row, :]

    def normalise(r):
        group_rows = 16

        def one(i, carry):
            at = pl.multiple_of(r * R + i * group_rows, group_rows)
            values = tok[pl.ds(at, group_rows), :].astype(f32)
            centered = values - jnp.mean(values, axis=1, keepdims=True)
            spread = jnp.mean(centered * centered, axis=1, keepdims=True)
            normed = centered * lax.rsqrt(spread + epsilon)
            to = pl.multiple_of(i * group_rows, group_rows)
            mod[pl.ds(to, group_rows), :] = (normed * table[0:1, :] + table[1:2, :]).astype(bf16)
            return carry

        lax.fori_loop(0, R // group_rows, one, 0)

    def compute(r):
        wait_mates(tok_copy, r)
        normalise(r)
        if r == 0:
            for i in range(kinds):
                w_twin_in(i).wait_recv()
        projected = jnp.dot(mod[...], wts[...], preferred_element_type=f32).astype(bf16)
        query[pl.ds(r * R, R), :] = projected[:, :size]
        kv[x, 0, pl.ds(r * R, R), :] = projected[:, size : 2 * size]
        kv[x, 1, pl.ds(r * R, R), :] = projected[:, 2 * size :]
        kv_copy(x, r).start()

    forwarded = 0
    for d in range(1, S):
        last = d == S - 1
        for r in range(chunks):
            relay(tok_copy, d, r)
            if r % 2 == 1 and forwarded < kinds:
                w_over_in(forwarded).wait_recv()
                w_twin(forwarded).start()
                forwarded += 1
            if last and r > 0:
                compute(r - 1)
        if d == S - 2:
            o_over(1 - x).wait_recv()
            local = pltpu.make_async_copy(o_src(own), o_at(own, g), local_sem.at[5])
            local.start()
            for step in range(1, slices):
                o_copy(step).start()
            local.wait()
            o_twin(own, g).start()

    compute(chunks - 1)
    for r in range(chunks):
        kv_copy(1 - x, r).wait_recv()

    factor = 1.0 / math.sqrt(size)
    contract = (((1,), (1,)), ((), ()))

    live = jnp.full((1, size), padded_smem[0], jnp.int32) < slices - own

    def attend(r):
        q = query[pl.ds(r * A, A), :]
        scores = [
            lax.dot_general(q, kv[b, 0], contract, preferred_element_type=f32) * factor for b in range(2)
        ]
        largest = jnp.maximum(
            jnp.max(scores[0], axis=1, keepdims=True), jnp.max(scores[1], axis=1, keepdims=True)
        )
        total, weighted = 0.0, 0.0
        for b in range(2):
            weights = jnp.exp(scores[b] - largest)
            total = total + jnp.sum(weights, axis=1, keepdims=True)
            weighted = weighted + jnp.dot(weights.astype(bf16), kv[b, 1], preferred_element_type=f32)
        attended = weighted / total
        masked = jnp.where(live, attended, 0.0).astype(bf16)
        att[pl.ds(r * A, A), lanes(own, size)] = masked
        send_own(att_copy, r)

    for r in range(pieces):
        attend(r)

    for step in range(1, slices):
        head = lax.rem(own + step, slices)
        o_in(head).wait_recv()
        o_twin(head, g).start()

    for d in range(1, S):
        for r in range(pieces):
            relay(att_copy, d, r)

    for head in range(slices):
        o_twin(head, 1 - g).wait_recv()
    gate = table[2:3, lanes(own, width)]
    weight = wout[...].reshape(slices * size, width)
    for r in range(pieces):
        wait_mates(att_copy, r)
        summed = jnp.dot(att[pl.ds(r * A, A), :], weight, preferred_element_type=f32)
        out_ref[pl.ds(r * A, A), :] = gate * summed

    drain(tok_copy, chunks)
    drain(att_copy, pieces)
    for i in range(kinds):
        w_over(i).wait_send()
        w_twin(i).wait_send()
    for r in range(chunks):
        kv_copy(x, r).wait_send()
    o_over(x).wait_send()
    for step in range(1, slices):
        o_copy(step).wait_send()
    for head in range(slices):
        o_twin(head, g).wait_send()


def fused_body(S, tokens, timestep, padded_heads, modulation, qkv_weight, out_weight):
    slices = 2 * S
    rows, width = tokens.shape
    kinds, half, size = qkv_weight.shape
    model_width = modulation.shape[2]
    chunks, pieces = 4, 2
    by_kind = jnp.transpose(modulation, (1, 0, 2))
    anywhere = pl.BlockSpec(memory_space=pltpu.HBM)
    vmem = pl.BlockSpec(memory_space=pltpu.VMEM)
    dma = pltpu.SemaphoreType.DMA
    update = pl.pallas_call(
        functools.partial(fused_kernel, (S, chunks, pieces)),
        out_shape=jax.ShapeDtypeStruct((rows, width), f32),
        in_specs=[anywhere] * 6,
        out_specs=vmem,
        scratch_shapes=[
            pltpu.SMEM((1,), jnp.int32),
            pltpu.SMEM((1,), jnp.int32),
            pltpu.VMEM(by_kind.shape, f32),
            pltpu.VMEM((rows, model_width), bf16),
            pltpu.VMEM((rows // chunks, model_width), bf16),
            pltpu.VMEM((model_width, kinds * size), bf16),
            pltpu.VMEM((rows, size), bf16),
            pltpu.VMEM((2, 2, rows, size), bf16),
            pltpu.VMEM((rows, slices * size), bf16),
            pltpu.VMEM((slices, size, width), bf16),
            pltpu.VMEM((2, size // 2, out_weight.shape[1]), bf16),
            pltpu.VMEM((8, model_width), f32),
            dma((10,)),
            dma((3, slices, chunks)),
            dma((slices, chunks)),
            dma((2, kinds)),
            dma((2, kinds)),
            dma((chunks,)),
            dma((chunks,)),
            dma((3, slices, pieces)),
            dma((slices, pieces)),
            dma((3, slices)),
            dma((3, slices)),
        ],
        compiler_params=pltpu.CompilerParams(collective_id=0, has_side_effects=True),
    )(tokens, timestep, padded_heads, by_kind, qkv_weight, out_weight)
    return update.astype(bf16)


def fits(mesh):
    shape = mesh.shape
    return shape["group"] == 2 and shape["blk"] == 2 and shape["tp"] == 2 and shape["seq"] >= 3


def solution(mesh):
    chosen = functools.partial(fused_body, mesh.shape["seq"]) if fits(mesh) else body
    return jax.shard_map(
        chosen,
        mesh=mesh,
        in_specs=(
            P(("group", "blk"), ("seq", "tp")),
            P("group"),
            P("group"),
            P(),
            P(None, "blk", ("seq", "tp")),
            P(("seq", "tp"), "blk"),
        ),
        out_specs=P(("group", "blk"), ("seq", "tp")),
        check_vma=False,
    )
```

```python
import functools
import math

import jax
import jax.numpy as jnp
from jax import lax
from jax.experimental import pallas as pl
from jax.experimental.pallas import tpu as pltpu
from jax.sharding import PartitionSpec as P

epsilon = 1e-06
neg_large = -1e30


def collect(own_part):
    gathered = lax.all_gather(own_part, ("seq", "tp"), axis=1, tiled=True)
    return gathered


def attend_block(running, queries, key_block, value_block, factor):
    largest, totals, weighted = running
    scores = (
        lax.dot_general(
            queries, key_block, (((1,), (1,)), ((), ())), preferred_element_type=jnp.float32
        )
        * factor
    )
    new_max = jnp.maximum(largest, jnp.max(scores, axis=1))
    rescale = jnp.exp(largest - new_max)
    weights = jnp.exp(scores - new_max[:, None])
    totals = totals * rescale + jnp.sum(weights, axis=1)
    weighted = weighted * rescale[:, None] + jnp.dot(
        weights.astype(jnp.bfloat16), value_block, preferred_element_type=jnp.float32
    )
    return (new_max, totals, weighted)


def body(tokens, timestep, padded_heads, modulation, qkv_weight, out_weight):
    slices = lax.axis_size(("seq", "tp"))
    own_index = lax.axis_index(("seq", "tp"))
    model_width = modulation.shape[2]
    own_width = model_width // slices
    token_rows = tokens.shape[0]
    head_size = out_weight.shape[0]
    table_row = lax.dynamic_index_in_dim(modulation, timestep[0], 0, keepdims=False)
    own_entry = lax.dynamic_slice_in_dim(table_row, own_index * own_width, own_width, 1)
    gathered = collect(tokens).astype(jnp.float32)
    average = jnp.mean(gathered, axis=1, keepdims=True)
    centered = gathered - average
    spread = jnp.mean(centered * centered, axis=1, keepdims=True)
    normed = centered * lax.rsqrt(spread + epsilon)
    modulated = (normed * (1.0 + table_row[1]) + table_row[0]).astype(jnp.bfloat16)
    projected = jnp.einsum(
        "td,kde->kte",
        modulated,
        lax.all_gather(qkv_weight, "blk", axis=1, tiled=True),
        preferred_element_type=jnp.float32,
    ).astype(jnp.bfloat16)
    queries = projected[0]
    factor = 1.0 / math.sqrt(head_size)
    initial = (
        jnp.full((token_rows,), neg_large, jnp.float32),
        jnp.zeros((token_rows,), jnp.float32),
        jnp.zeros((token_rows, head_size), jnp.float32),
    )
    key_piece = lax.all_gather(projected[1], "blk", axis=0, tiled=True)
    value_piece = lax.all_gather(projected[2], "blk", axis=0, tiled=True)
    length = key_piece.shape[0]

    def one_block(counter, inner_state):
        key_block = lax.dynamic_slice_in_dim(key_piece, counter * 512, 512, 0)
        value_block = lax.dynamic_slice_in_dim(value_piece, counter * 512, 512, 0)
        return attend_block(inner_state, queries, key_block, value_block, factor)

    largest, exp_totals, weighted = lax.fori_loop(0, length // 512, one_block, initial)
    attended = weighted / exp_totals[:, None]
    live_heads = slices - padded_heads[0]
    masked = jnp.where(own_index < live_heads, attended, 0.0).astype(jnp.bfloat16)
    head_term = jnp.dot(
        masked,
        lax.all_gather(out_weight, "blk", axis=1, tiled=True),
        preferred_element_type=jnp.float32,
    )
    summed = lax.psum_scatter(
        head_term.astype(jnp.bfloat16), ("seq", "tp"), scatter_dimension=1, tiled=True
    ).astype(jnp.float32)
    return (own_entry[2] * summed).astype(jnp.bfloat16)


MESH = pl.DeviceIdType.MESH
bf16, f32 = jnp.bfloat16, jnp.float32


def fused_kernel(
    dims,
    tokens_ref,
    step_ref,
    padded_ref,
    modulation_ref,
    qkv_ref,
    out_weight_ref,
    out_ref,
    step_smem,
    padded_smem,
    modulation,
    tok,
    mod,
    wts,
    query,
    kv,
    att,
    wout,
    outw,
    table,
    lift,
    vectors,
    level,
    sums,
    squares,
    total,
    local_sem,
    tok_send,
    tok_recv,
    w_send,
    w_recv,
    kv_send,
    kv_recv,
    att_send,
    att_recv,
    o_send,
    o_recv,
):
    S, chunks, pieces = dims
    rows, width = tokens_ref.shape
    kinds, half, size = qkv_ref.shape
    slices = 2 * S
    g, z = lax.axis_index("group"), lax.axis_index("seq")
    x, c = lax.axis_index("blk"), lax.axis_index("tp")
    own = z * 2 + c
    R = rows // chunks
    A = rows // pieces
    part = half // 2
    hpart = size // 2

    up, down = (g, z + 1, x, c), (g, z - 1, x, c)
    mate = (g, z, x, 1 - c)
    over = (g, z, 1 - x, c)
    twin = (1 - g, z, x, c)

    def remote(src, dst, s_sem, r_sem, where):
        return pltpu.make_async_remote_copy(
            src_ref=src,
            dst_ref=dst,
            send_sem=s_sem,
            recv_sem=r_sem,
            device_id=where,
            device_id_type=MESH,
        )

    def lanes(index, extent):
        return pl.ds(pl.multiple_of(index * extent, 128), extent)

    def tok_at(s, r):
        return tok.at[pl.ds(r * R, R), lanes(s, width)]

    def att_at(s, r):
        return att.at[pl.ds(r * A, A), lanes(s, size)]

    def tok_copy(way, s, r, where, src=None):
        there = tok_at(s, r)
        return remote(there if src is None else src, there, tok_send.at[way, s, r], tok_recv.at[s, r], where)

    def att_copy(way, s, r, where, src=None):
        there = att_at(s, r)
        return remote(there, there, att_send.at[way, s, r], att_recv.at[s, r], where)

    def send_own(make, r, src=None):
        @pl.when(z < S - 1)
        def _():
            make(0, own, r, up, src).start()

        @pl.when(z > 0)
        def _():
            make(1, own, r, down, src).start()

        make(2, own, r, mate, src).start()

    def relay(make, d, r):
        @pl.when(z - d >= 0)
        def _():
            s = (z - d) * 2 + c
            make(0, s, r, up).wait_recv()

            @pl.when(z < S - 1)
            def _():
                make(0, s, r, up).start()

            make(2, s, r, mate).start()

        @pl.when(z + d < S)
        def _():
            s = (z + d) * 2 + c
            make(1, s, r, down).wait_recv()

            @pl.when(z > 0)
            def _():
                make(1, s, r, down).start()

            make(2, s, r, mate).start()

    def wait_mates(make, r):
        for other in range(S):
            make(2, other * 2 + 1 - c, r, mate).wait_recv()

    def drain(make, count):
        for r in range(count):
            for other in range(S):
                s = other * 2 + c

                @pl.when((z < S - 1) & (other <= z))
                def _():
                    make(0, s, r, up).wait_send()

                @pl.when((z > 0) & (other >= z))
                def _():
                    make(1, s, r, down).wait_send()

                make(2, s, r, mate).wait_send()

    def w_at(block, p, i):
        first = pl.multiple_of(block * half + p * part, 16)
        return wts.at[pl.ds(first, part), pl.ds(i * size, size)]

    def w_over(i):
        src = qkv_ref.at[i, pl.ds(pl.multiple_of(g * part, 16), part)]
        return remote(src, w_at(x, g, i), w_send.at[0, i], w_recv.at[0, i], over)

    def w_over_in(i):
        there = w_at(1 - x, g, i)
        return remote(there, there, w_send.at[0, i], w_recv.at[0, i], over)

    def w_twin(i):
        there = w_at(1 - x, g, i)
        return remote(there, there, w_send.at[1, i], w_recv.at[1, i], twin)

    def w_twin_in(i):
        there = w_at(1 - x, 1 - g, i)
        return remote(there, there, w_send.at[1, i], w_recv.at[1, i], twin)

    def o_at(head, p):
        return wout.at[head, pl.ds(pl.multiple_of(p * hpart, 16), hpart)]

    def o_over(block):
        src = out_weight_ref.at[pl.ds(pl.multiple_of(g * hpart, 16), hpart)]
        return remote(src, outw.at[block], o_send.at[0, 0], o_recv.at[0, 0], over)

    per_blk = slices // 2

    def o_src(s):
        return outw.at[s // per_blk, :, lanes(lax.rem(s, per_blk), width)]

    def o_copy(step):
        s = lax.rem(own + step, slices)
        return remote(o_src(s), o_at(own, g), o_send.at[1, step], o_recv.at[1, own], (g, s // 2, x, s % 2))

    def o_in(head):
        return remote(o_at(head, g), o_at(head, g), o_send.at[1, 0], o_recv.at[1, head], mate)

    def o_twin(head, p):
        return remote(o_at(head, p), o_at(head, p), o_send.at[2, head], o_recv.at[2, head], twin)

    def kv_at(block, r):
        return kv.at[block, :, pl.ds(r * R, R)]

    def kv_copy(block, r):
        return remote(kv_at(block, r), kv_at(block, r), kv_send.at[r], kv_recv.at[r], over)

    barrier = pltpu.get_barrier_semaphore()
    for step in range(1, slices):
        s = lax.rem(own + step, slices)
        pl.semaphore_signal(barrier, inc=1, device_id=(g, s // 2, x, s % 2), device_id_type=MESH)
    for where in (over, twin):
        pl.semaphore_signal(barrier, inc=1, device_id=where, device_id_type=MESH)
    locals_ = [
        pltpu.make_async_copy(tokens_ref, tok.at[:, lanes(own, width)], local_sem.at[0]),
        pltpu.make_async_copy(step_ref, step_smem, local_sem.at[6]),
        pltpu.make_async_copy(padded_ref, padded_smem, local_sem.at[7]),
        pltpu.make_async_copy(modulation_ref, modulation, local_sem.at[8]),
        pltpu.make_async_copy(
            out_weight_ref.at[pl.ds(pl.multiple_of(g * hpart, 16), hpart)], outw.at[x], local_sem.at[9]
        ),
    ]
    for i in range(kinds):
        there = wts.at[pl.ds(pl.multiple_of(x * half, 16), half), pl.ds(i * size, size)]
        locals_.append(pltpu.make_async_copy(qkv_ref.at[i], there, local_sem.at[1 + i]))
    for copy in locals_:
        copy.start()
    pl.semaphore_wait(barrier, slices + 1)

    for r in range(chunks):
        send_own(tok_copy, r, tokens_ref.at[pl.ds(r * R, R)])
    for i in range(kinds):
        w_over(i).start()
    o_over(x).start()
    for copy in locals_:
        copy.wait()
    row = pl.ds(step_smem[0], 1)
    table[0:1, :] = 1.0 + modulation[1, row, :]
    table[1:2, :] = modulation[0, row, :]
    table[2:3, :] = modulation[2, row, :]

    block = 32
    span = 2 * width
    tile = level.shape[1]

    def fold(values):
        folded = values[:, :tile]
        for i in range(1, values.shape[1] // tile):
            folded = folded + values[:, i * tile : (i + 1) * tile]
        return folded

    def set_level(i, carry):
        at = pl.ds(pl.multiple_of(i * block, block), block)
        values = tok[at, lanes(own, width)].astype(f32)
        level[at, :] = jnp.broadcast_to(jnp.mean(values, axis=1, keepdims=True), (block, tile))
        return carry

    lax.fori_loop(0, rows // block, set_level, 0)
    lift[...] = jnp.zeros_like(lift)
    for i in range(2):
        high = table[i : i + 1, :].astype(bf16).astype(f32)
        lift[2 * i : 2 * i + 1, :] = high
        lift[2 * i + 1 : 2 * i + 2, :] = table[i : i + 1, :] - high

    def set_vectors():
        for i in range(kinds):
            w_twin_in(i).wait_recv()
        product = jnp.dot(lift[...].astype(bf16), wts[...], preferred_element_type=f32)
        vectors[0:1, :] = product[0:1] + product[1:2]
        vectors[1:2, :] = product[2:3] + product[3:4]

    def add_pair(chip, r, count, first=False):
        for i in range(r, r + count):
            tok_copy(2, chip * 2 + 1 - c, i, mate).wait_recv()
        columns = lanes(chip, span)

        def one(i, carry):
            at = pl.ds(pl.multiple_of(r * R + i * block, block), block)
            base = level[at, :]
            shifted = tok[at, columns].astype(f32) - jnp.concatenate([base] * (span // tile), axis=1)
            if first:
                sums[at, :] = fold(shifted)
                squares[at, :] = fold(shifted * shifted)
            else:
                sums[at, :] += fold(shifted)
                squares[at, :] += fold(shifted * shifted)
            mod[pl.ds(pl.multiple_of(i * block, block), block), :] = (shifted * table[0:1, columns]).astype(bf16)
            return carry

        lax.fori_loop(0, count * R // block, one, 0)
        depth = pl.ds(pl.multiple_of(chip * span, 16), span)
        at = pl.ds(r * R, count * R)
        product = jnp.dot(mod[: count * R, :], wts[depth, :], preferred_element_type=f32)
        total[at, :] = product if first else total[at, :] + product

    def add_ring(d, r, count):
        @pl.when(z - d >= 0)
        def _():
            add_pair(z - d, r, count)

        @pl.when(z + d < S)
        def _():
            add_pair(z + d, r, count)

    def finish(r):
        at = pl.ds(r * R, R)
        share = 1.0 / (slices * width)
        offset = jnp.sum(sums[at, :], axis=1, keepdims=True) * share
        spread = jnp.sum(squares[at, :], axis=1, keepdims=True) * share - offset * offset
        rate = lax.rsqrt(jnp.maximum(spread, 0.0) + epsilon)
        projected = ((total[at, :] - offset * vectors[0:1, :]) * rate + vectors[1:2, :]).astype(bf16)
        query[at, :] = projected[:, :size]
        kv[x, 0, at, :] = projected[:, size : 2 * size]
        kv[x, 1, at, :] = projected[:, 2 * size :]
        kv_copy(x, r).start()

    forwarded = 0
    for d in range(1, S):
        last = d == S - 1
        for r in range(chunks):
            relay(tok_copy, d, r)
            if r % 2 == 1 and forwarded < kinds:
                w_over_in(forwarded).wait_recv()
                w_twin(forwarded).start()
                forwarded += 1
            if last:
                add_ring(d - 1, r, 1)
                if r > 0:
                    add_ring(d, r - 1, 1)
                    finish(r - 1)
        if d == S - 2:
            set_vectors()
            for r in range(0, chunks, 2):
                add_pair(z, r, 2, True)
            for near in range(1, d):
                for r in range(0, chunks, 2):
                    add_ring(near, r, 2)

    o_over(1 - x).wait_recv()
    local = pltpu.make_async_copy(o_src(own), o_at(own, g), local_sem.at[5])
    local.start()
    for step in range(1, slices):
        o_copy(step).start()
    add_ring(S - 1, chunks - 1, 1)
    finish(chunks - 1)
    local.wait()
    o_twin(own, g).start()

    for r in range(chunks):
        kv_copy(1 - x, r).wait_recv()

    factor = 1.0 / math.sqrt(size)
    contract = (((1,), (1,)), ((), ()))

    live = jnp.full((1, size), padded_smem[0], jnp.int32) < slices - own

    def attend(r):
        q = query[pl.ds(r * A, A), :]
        scores = [
            lax.dot_general(q, kv[b, 0], contract, preferred_element_type=f32) * factor for b in range(2)
        ]
        largest = jnp.maximum(
            jnp.max(scores[0], axis=1, keepdims=True), jnp.max(scores[1], axis=1, keepdims=True)
        )
        total, weighted = 0.0, 0.0
        for b in range(2):
            weights = jnp.exp(scores[b] - largest)
            total = total + jnp.sum(weights, axis=1, keepdims=True)
            weighted = weighted + jnp.dot(weights.astype(bf16), kv[b, 1], preferred_element_type=f32)
        attended = weighted / total
        masked = jnp.where(live, attended, 0.0).astype(bf16)
        att[pl.ds(r * A, A), lanes(own, size)] = masked
        send_own(att_copy, r)

    for r in range(pieces):
        attend(r)

    for d in range(1, S):
        for r in range(pieces):
            relay(att_copy, d, r)
        if d == 1:
            for step in range(1, slices):
                head = lax.rem(own + step, slices)
                o_in(head).wait_recv()
                o_twin(head, g).start()

    for head in range(slices):
        o_twin(head, 1 - g).wait_recv()
    gate = table[2:3, lanes(own, width)]
    weight = wout[...].reshape(slices * size, width)
    for r in range(pieces):
        wait_mates(att_copy, r)
        summed = jnp.dot(att[pl.ds(r * A, A), :], weight, preferred_element_type=f32)
        out_ref[pl.ds(r * A, A), :] = gate * summed

    drain(tok_copy, chunks)
    drain(att_copy, pieces)
    for i in range(kinds):
        w_over(i).wait_send()
        w_twin(i).wait_send()
    for r in range(chunks):
        kv_copy(x, r).wait_send()
    o_over(x).wait_send()
    for step in range(1, slices):
        o_copy(step).wait_send()
    for head in range(slices):
        o_twin(head, g).wait_send()


def fused_body(S, tokens, timestep, padded_heads, modulation, qkv_weight, out_weight):
    slices = 2 * S
    rows, width = tokens.shape
    kinds, half, size = qkv_weight.shape
    model_width = modulation.shape[2]
    chunks, pieces = 4, 2
    by_kind = jnp.transpose(modulation, (1, 0, 2))
    anywhere = pl.BlockSpec(memory_space=pltpu.HBM)
    vmem = pl.BlockSpec(memory_space=pltpu.VMEM)
    dma = pltpu.SemaphoreType.DMA
    update = pl.pallas_call(
        functools.partial(fused_kernel, (S, chunks, pieces)),
        out_shape=jax.ShapeDtypeStruct((rows, width), f32),
        in_specs=[anywhere] * 6,
        out_specs=vmem,
        scratch_shapes=[
            pltpu.SMEM((1,), jnp.int32),
            pltpu.SMEM((1,), jnp.int32),
            pltpu.VMEM(by_kind.shape, f32),
            pltpu.VMEM((rows, model_width), bf16),
            pltpu.VMEM((2 * rows // chunks, 2 * width), bf16),
            pltpu.VMEM((model_width, kinds * size), bf16),
            pltpu.VMEM((rows, size), bf16),
            pltpu.VMEM((2, 2, rows, size), bf16),
            pltpu.VMEM((rows, slices * size), bf16),
            pltpu.VMEM((slices, size, width), bf16),
            pltpu.VMEM((2, size // 2, out_weight.shape[1]), bf16),
            pltpu.VMEM((8, model_width), f32),
            pltpu.VMEM((8, model_width), f32),
            pltpu.VMEM((8, kinds * size), f32),
            pltpu.VMEM((rows, 128), f32),
            pltpu.VMEM((rows, 128), f32),
            pltpu.VMEM((rows, 128), f32),
            pltpu.VMEM((rows, kinds * size), f32),
            dma((10,)),
            dma((3, slices, chunks)),
            dma((slices, chunks)),
            dma((2, kinds)),
            dma((2, kinds)),
            dma((chunks,)),
            dma((chunks,)),
            dma((3, slices, pieces)),
            dma((slices, pieces)),
            dma((3, slices)),
            dma((3, slices)),
        ],
        compiler_params=pltpu.CompilerParams(collective_id=0, has_side_effects=True),
    )(tokens, timestep, padded_heads, by_kind, qkv_weight, out_weight)
    return update.astype(bf16)


def fits(mesh):
    shape = mesh.shape
    return shape["group"] == 2 and shape["blk"] == 2 and shape["tp"] == 2 and shape["seq"] >= 4


def solution(mesh):
    chosen = functools.partial(fused_body, mesh.shape["seq"]) if fits(mesh) else body
    return jax.shard_map(
        chosen,
        mesh=mesh,
        in_specs=(
            P(("group", "blk"), ("seq", "tp")),
            P("group"),
            P("group"),
            P(),
            P(None, "blk", ("seq", "tp")),
            P(("seq", "tp"), "blk"),
        ),
        out_specs=P(("group", "blk"), ("seq", "tp")),
        check_vma=False,
    )
```

```python
import functools
import math

import jax
import jax.numpy as jnp
from jax import lax
from jax.experimental import pallas as pl
from jax.experimental.pallas import tpu as pltpu
from jax.sharding import PartitionSpec as P

epsilon = 1e-06
neg_large = -1e30


def collect(own_part):
    gathered = lax.all_gather(own_part, ("seq", "tp"), axis=1, tiled=True)
    return gathered


def attend_block(running, queries, key_block, value_block, factor):
    largest, totals, weighted = running
    scores = (
        lax.dot_general(
            queries, key_block, (((1,), (1,)), ((), ())), preferred_element_type=jnp.float32
        )
        * factor
    )
    new_max = jnp.maximum(largest, jnp.max(scores, axis=1))
    rescale = jnp.exp(largest - new_max)
    weights = jnp.exp(scores - new_max[:, None])
    totals = totals * rescale + jnp.sum(weights, axis=1)
    weighted = weighted * rescale[:, None] + jnp.dot(
        weights.astype(jnp.bfloat16), value_block, preferred_element_type=jnp.float32
    )
    return (new_max, totals, weighted)


def body(tokens, timestep, padded_heads, modulation, qkv_weight, out_weight):
    slices = lax.axis_size(("seq", "tp"))
    own_index = lax.axis_index(("seq", "tp"))
    model_width = modulation.shape[2]
    own_width = model_width // slices
    token_rows = tokens.shape[0]
    head_size = out_weight.shape[0]
    table_row = lax.dynamic_index_in_dim(modulation, timestep[0], 0, keepdims=False)
    own_entry = lax.dynamic_slice_in_dim(table_row, own_index * own_width, own_width, 1)
    gathered = collect(tokens).astype(jnp.float32)
    average = jnp.mean(gathered, axis=1, keepdims=True)
    centered = gathered - average
    spread = jnp.mean(centered * centered, axis=1, keepdims=True)
    normed = centered * lax.rsqrt(spread + epsilon)
    modulated = (normed * (1.0 + table_row[1]) + table_row[0]).astype(jnp.bfloat16)
    projected = jnp.einsum(
        "td,kde->kte",
        modulated,
        lax.all_gather(qkv_weight, "blk", axis=1, tiled=True),
        preferred_element_type=jnp.float32,
    ).astype(jnp.bfloat16)
    queries = projected[0]
    factor = 1.0 / math.sqrt(head_size)
    initial = (
        jnp.full((token_rows,), neg_large, jnp.float32),
        jnp.zeros((token_rows,), jnp.float32),
        jnp.zeros((token_rows, head_size), jnp.float32),
    )
    key_piece = lax.all_gather(projected[1], "blk", axis=0, tiled=True)
    value_piece = lax.all_gather(projected[2], "blk", axis=0, tiled=True)
    length = key_piece.shape[0]

    def one_block(counter, inner_state):
        key_block = lax.dynamic_slice_in_dim(key_piece, counter * 512, 512, 0)
        value_block = lax.dynamic_slice_in_dim(value_piece, counter * 512, 512, 0)
        return attend_block(inner_state, queries, key_block, value_block, factor)

    largest, exp_totals, weighted = lax.fori_loop(0, length // 512, one_block, initial)
    attended = weighted / exp_totals[:, None]
    live_heads = slices - padded_heads[0]
    masked = jnp.where(own_index < live_heads, attended, 0.0).astype(jnp.bfloat16)
    head_term = jnp.dot(
        masked,
        lax.all_gather(out_weight, "blk", axis=1, tiled=True),
        preferred_element_type=jnp.float32,
    )
    summed = lax.psum_scatter(
        head_term.astype(jnp.bfloat16), ("seq", "tp"), scatter_dimension=1, tiled=True
    ).astype(jnp.float32)
    return (own_entry[2] * summed).astype(jnp.bfloat16)


MESH = pl.DeviceIdType.MESH
bf16, f32 = jnp.bfloat16, jnp.float32


def fused_kernel(
    dims,
    tokens_ref,
    step_ref,
    padded_ref,
    modulation_ref,
    qkv_ref,
    out_weight_ref,
    out_ref,
    step_smem,
    padded_smem,
    modulation,
    tok,
    mod,
    wts,
    query,
    kv,
    att,
    wout,
    outw,
    table,
    lift,
    vectors,
    level,
    sums,
    squares,
    total,
    local_sem,
    tok_send,
    tok_recv,
    w_send,
    w_recv,
    kv_send,
    kv_recv,
    att_send,
    att_recv,
    o_send,
    o_recv,
):
    S, chunks, pieces = dims
    rows, width = tokens_ref.shape
    kinds, half, size = qkv_ref.shape
    slices = 2 * S
    g, z = lax.axis_index("group"), lax.axis_index("seq")
    x, c = lax.axis_index("blk"), lax.axis_index("tp")
    own = z * 2 + c
    R = rows // chunks
    A = rows // pieces
    part = half // 2
    hpart = size // 2

    up, down = (g, z + 1, x, c), (g, z - 1, x, c)
    mate = (g, z, x, 1 - c)
    over = (g, z, 1 - x, c)
    twin = (1 - g, z, x, c)

    def remote(src, dst, s_sem, r_sem, where):
        return pltpu.make_async_remote_copy(
            src_ref=src,
            dst_ref=dst,
            send_sem=s_sem,
            recv_sem=r_sem,
            device_id=where,
            device_id_type=MESH,
        )

    def lanes(index, extent):
        return pl.ds(pl.multiple_of(index * extent, 128), extent)

    def tok_at(s, r):
        return tok.at[pl.ds(r * R, R), lanes(s, width)]

    def att_at(s, r):
        return att.at[pl.ds(r * A, A), lanes(s, size)]

    def tok_copy(way, s, r, where, src=None):
        there = tok_at(s, r)
        return remote(there if src is None else src, there, tok_send.at[way, s, r], tok_recv.at[s, r], where)

    def att_copy(way, s, r, where, src=None):
        there = att_at(s, r)
        return remote(there, there, att_send.at[way, s, r], att_recv.at[s, r], where)

    def send_own(make, r, src=None):
        @pl.when(z < S - 1)
        def _():
            make(0, own, r, up, src).start()

        @pl.when(z > 0)
        def _():
            make(1, own, r, down, src).start()

        make(2, own, r, mate, src).start()

    def relay(make, d, r):
        @pl.when(z - d >= 0)
        def _():
            s = (z - d) * 2 + c
            make(0, s, r, up).wait_recv()

            @pl.when(z < S - 1)
            def _():
                make(0, s, r, up).start()

            make(2, s, r, mate).start()

        @pl.when(z + d < S)
        def _():
            s = (z + d) * 2 + c
            make(1, s, r, down).wait_recv()

            @pl.when(z > 0)
            def _():
                make(1, s, r, down).start()

            make(2, s, r, mate).start()

    def wait_mates(make, r):
        for other in range(S):
            make(2, other * 2 + 1 - c, r, mate).wait_recv()

    def drain(make, count):
        for r in range(count):
            for other in range(S):
                s = other * 2 + c

                @pl.when((z < S - 1) & (other <= z))
                def _():
                    make(0, s, r, up).wait_send()

                @pl.when((z > 0) & (other >= z))
                def _():
                    make(1, s, r, down).wait_send()

                make(2, s, r, mate).wait_send()

    def w_at(block, p, i):
        first = pl.multiple_of(block * half + p * part, 16)
        return wts.at[pl.ds(first, part), pl.ds(i * size, size)]

    def w_over(i):
        src = qkv_ref.at[i, pl.ds(pl.multiple_of(g * part, 16), part)]
        return remote(src, w_at(x, g, i), w_send.at[0, i], w_recv.at[0, i], over)

    def w_over_in(i):
        there = w_at(1 - x, g, i)
        return remote(there, there, w_send.at[0, i], w_recv.at[0, i], over)

    def w_twin(i):
        there = w_at(1 - x, g, i)
        return remote(there, there, w_send.at[1, i], w_recv.at[1, i], twin)

    def w_twin_in(i):
        there = w_at(1 - x, 1 - g, i)
        return remote(there, there, w_send.at[1, i], w_recv.at[1, i], twin)

    def o_at(head, p):
        return wout.at[head, pl.ds(pl.multiple_of(p * hpart, 16), hpart)]

    def o_over(block):
        src = out_weight_ref.at[pl.ds(pl.multiple_of(g * hpart, 16), hpart)]
        return remote(src, outw.at[block], o_send.at[0, 0], o_recv.at[0, 0], over)

    per_blk = slices // 2

    def o_src(s):
        return outw.at[s // per_blk, :, lanes(lax.rem(s, per_blk), width)]

    def o_copy(step):
        s = lax.rem(own + step, slices)
        return remote(o_src(s), o_at(own, g), o_send.at[1, step], o_recv.at[1, own], (g, s // 2, x, s % 2))

    def o_in(head):
        return remote(o_at(head, g), o_at(head, g), o_send.at[1, 0], o_recv.at[1, head], mate)

    def o_twin(head, p):
        return remote(o_at(head, p), o_at(head, p), o_send.at[2, head], o_recv.at[2, head], twin)

    def kv_at(block, r):
        return kv.at[block, :, pl.ds(r * R, R)]

    def kv_copy(block, r):
        return remote(kv_at(block, r), kv_at(block, r), kv_send.at[r], kv_recv.at[r], over)

    barrier = pltpu.get_barrier_semaphore()
    for step in range(1, slices):
        s = lax.rem(own + step, slices)
        pl.semaphore_signal(barrier, inc=1, device_id=(g, s // 2, x, s % 2), device_id_type=MESH)
    for where in (over, twin):
        pl.semaphore_signal(barrier, inc=1, device_id=where, device_id_type=MESH)
    locals_ = [
        pltpu.make_async_copy(tokens_ref, tok.at[:, lanes(own, width)], local_sem.at[0]),
        pltpu.make_async_copy(step_ref, step_smem, local_sem.at[6]),
        pltpu.make_async_copy(padded_ref, padded_smem, local_sem.at[7]),
        pltpu.make_async_copy(modulation_ref, modulation, local_sem.at[8]),
        pltpu.make_async_copy(
            out_weight_ref.at[pl.ds(pl.multiple_of(g * hpart, 16), hpart)], outw.at[x], local_sem.at[9]
        ),
    ]
    for i in range(kinds):
        there = wts.at[pl.ds(pl.multiple_of(x * half, 16), half), pl.ds(i * size, size)]
        locals_.append(pltpu.make_async_copy(qkv_ref.at[i], there, local_sem.at[1 + i]))
    for copy in locals_:
        copy.start()
    pl.semaphore_wait(barrier, slices + 1)

    for r in range(chunks):
        send_own(tok_copy, r, tokens_ref.at[pl.ds(r * R, R)])
    for i in range(kinds):
        w_over(i).start()
    o_over(x).start()
    for copy in locals_:
        copy.wait()
    row = pl.ds(step_smem[0], 1)
    table[0:1, :] = 1.0 + modulation[1, row, :]
    table[1:2, :] = modulation[0, row, :]
    table[2:3, :] = modulation[2, row, :]

    block = 32
    span = 2 * width
    tile = level.shape[1]

    def fold(values):
        folded = values[:, :tile]
        for i in range(1, values.shape[1] // tile):
            folded = folded + values[:, i * tile : (i + 1) * tile]
        return folded

    def set_level(i, carry):
        at = pl.ds(pl.multiple_of(i * block, block), block)
        values = tok[at, lanes(own, width)].astype(f32)
        level[at, :] = jnp.broadcast_to(jnp.mean(values, axis=1, keepdims=True), (block, tile))
        return carry

    lax.fori_loop(0, rows // block, set_level, 0)
    lift[...] = jnp.zeros_like(lift)
    for i in range(2):
        high = table[i : i + 1, :].astype(bf16).astype(f32)
        lift[2 * i : 2 * i + 1, :] = high
        lift[2 * i + 1 : 2 * i + 2, :] = table[i : i + 1, :] - high

    def set_vectors():
        for i in range(kinds):
            w_twin_in(i).wait_recv()
        product = jnp.dot(lift[...].astype(bf16), wts[...], preferred_element_type=f32)
        vectors[0:1, :] = product[0:1] + product[1:2]
        vectors[1:2, :] = product[2:3] + product[3:4]

    def add_pair(chip, r, count, first=False):
        for i in range(r, r + count):
            tok_copy(2, chip * 2 + 1 - c, i, mate).wait_recv()
        columns = lanes(chip, span)

        def one(i, carry):
            at = pl.ds(pl.multiple_of(r * R + i * block, block), block)
            base = level[at, :]
            shifted = tok[at, columns].astype(f32) - jnp.concatenate([base] * (span // tile), axis=1)
            if first:
                sums[at, :] = fold(shifted)
                squares[at, :] = fold(shifted * shifted)
            else:
                sums[at, :] += fold(shifted)
                squares[at, :] += fold(shifted * shifted)
            mod[pl.ds(pl.multiple_of(i * block, block), block), :] = (shifted * table[0:1, columns]).astype(bf16)
            return carry

        lax.fori_loop(0, count * R // block, one, 0)
        depth = pl.ds(pl.multiple_of(chip * span, 16), span)
        at = pl.ds(r * R, count * R)
        product = jnp.dot(mod[: count * R, :], wts[depth, :], preferred_element_type=f32)
        total[at, :] = product if first else total[at, :] + product

    def add_ring(d, r, count):
        @pl.when(z - d >= 0)
        def _():
            add_pair(z - d, r, count)

        @pl.when(z + d < S)
        def _():
            add_pair(z + d, r, count)

    def finish(r):
        at = pl.ds(r * R, R)
        share = 1.0 / (slices * width)
        offset = jnp.sum(sums[at, :], axis=1, keepdims=True) * share
        spread = jnp.sum(squares[at, :], axis=1, keepdims=True) * share - offset * offset
        rate = lax.rsqrt(jnp.maximum(spread, 0.0) + epsilon)
        projected = ((total[at, :] - offset * vectors[0:1, :]) * rate + vectors[1:2, :]).astype(bf16)
        query[at, :] = projected[:, :size]
        kv[x, 0, at, :] = projected[:, size : 2 * size]
        kv[x, 1, at, :] = projected[:, 2 * size :]
        kv_copy(x, r).start()

    def send_out_weight(inner):
        for step in range(1, slices):
            chip = lax.rem(own + step, slices) // 2

            @pl.when(((chip > 0) & (chip < S - 1)) == inner)
            def _():
                o_copy(step).start()

    forwarded = 0
    for d in range(1, S):
        last = d == S - 1
        for r in range(chunks):
            relay(tok_copy, d, r)
            if r % 2 == 1 and forwarded < kinds:
                w_over_in(forwarded).wait_recv()
                w_twin(forwarded).start()
                forwarded += 1
            if last:
                add_ring(d - 1, r, 1)
                if r > 0:
                    add_ring(d, r - 1, 1)
                    finish(r - 1)
        if d == S - 2:
            set_vectors()
            o_over(1 - x).wait_recv()
            local = pltpu.make_async_copy(o_src(own), o_at(own, g), local_sem.at[5])
            local.start()
            send_out_weight(True)
            for r in range(0, chunks, 2):
                add_pair(z, r, 2, True)
            for near in range(1, d):
                for r in range(0, chunks, 2):
                    add_ring(near, r, 2)

    send_out_weight(False)
    add_ring(S - 1, chunks - 1, 1)
    finish(chunks - 1)
    local.wait()
    o_twin(own, g).start()

    factor = 1.0 / math.sqrt(size)
    contract = (((1,), (1,)), ((), ()))

    live = jnp.full((1, size), padded_smem[0], jnp.int32) < slices - own

    def attend(r):
        q = query[pl.ds(r * A, A), :]
        scores = []
        for b in (x, 1 - x):
            if r == 0 and len(scores) > 0:
                for i in range(chunks):
                    kv_copy(1 - x, i).wait_recv()
            scores.append(lax.dot_general(q, kv[b, 0], contract, preferred_element_type=f32) * factor)
        largest = jnp.maximum(
            jnp.max(scores[0], axis=1, keepdims=True), jnp.max(scores[1], axis=1, keepdims=True)
        )
        total, weighted = 0.0, 0.0
        for b, part_scores in zip((x, 1 - x), scores):
            weights = jnp.exp(part_scores - largest)
            total = total + jnp.sum(weights, axis=1, keepdims=True)
            weighted = weighted + jnp.dot(weights.astype(bf16), kv[b, 1], preferred_element_type=f32)
        attended = weighted / total
        masked = jnp.where(live, attended, 0.0).astype(bf16)
        att[pl.ds(r * A, A), lanes(own, size)] = masked
        send_own(att_copy, r)

    for r in range(pieces):
        attend(r)

    for d in range(1, S):
        for r in range(pieces):
            relay(att_copy, d, r)
        if d == 1:
            for step in range(1, slices):
                head = lax.rem(own + step, slices)
                o_in(head).wait_recv()
                o_twin(head, g).start()

    for head in range(slices):
        o_twin(head, 1 - g).wait_recv()
    gate = table[2:3, lanes(own, width)]
    weight = wout[...].reshape(slices * size, width)
    for r in range(pieces):
        wait_mates(att_copy, r)
        summed = jnp.dot(att[pl.ds(r * A, A), :], weight, preferred_element_type=f32)
        out_ref[pl.ds(r * A, A), :] = (gate * summed).astype(bf16)

    drain(tok_copy, chunks)
    drain(att_copy, pieces)
    for i in range(kinds):
        w_over(i).wait_send()
        w_twin(i).wait_send()
    for r in range(chunks):
        kv_copy(x, r).wait_send()
    o_over(x).wait_send()
    for step in range(1, slices):
        o_copy(step).wait_send()
    for head in range(slices):
        o_twin(head, g).wait_send()


def fused_body(S, tokens, timestep, padded_heads, modulation, qkv_weight, out_weight):
    slices = 2 * S
    rows, width = tokens.shape
    kinds, half, size = qkv_weight.shape
    model_width = modulation.shape[2]
    chunks, pieces = 4, 4
    by_kind = jnp.transpose(modulation, (1, 0, 2))
    anywhere = pl.BlockSpec(memory_space=pltpu.HBM)
    vmem = pl.BlockSpec(memory_space=pltpu.VMEM)
    dma = pltpu.SemaphoreType.DMA
    return pl.pallas_call(
        functools.partial(fused_kernel, (S, chunks, pieces)),
        out_shape=jax.ShapeDtypeStruct((rows, width), bf16),
        in_specs=[anywhere] * 6,
        out_specs=vmem,
        scratch_shapes=[
            pltpu.SMEM((1,), jnp.int32),
            pltpu.SMEM((1,), jnp.int32),
            pltpu.VMEM(by_kind.shape, f32),
            pltpu.VMEM((rows, model_width), bf16),
            pltpu.VMEM((2 * rows // chunks, 2 * width), bf16),
            pltpu.VMEM((model_width, kinds * size), bf16),
            pltpu.VMEM((rows, size), bf16),
            pltpu.VMEM((2, 2, rows, size), bf16),
            pltpu.VMEM((rows, slices * size), bf16),
            pltpu.VMEM((slices, size, width), bf16),
            pltpu.VMEM((2, size // 2, out_weight.shape[1]), bf16),
            pltpu.VMEM((8, model_width), f32),
            pltpu.VMEM((8, model_width), f32),
            pltpu.VMEM((8, kinds * size), f32),
            pltpu.VMEM((rows, 128), f32),
            pltpu.VMEM((rows, 128), f32),
            pltpu.VMEM((rows, 128), f32),
            pltpu.VMEM((rows, kinds * size), f32),
            dma((10,)),
            dma((3, slices, chunks)),
            dma((slices, chunks)),
            dma((2, kinds)),
            dma((2, kinds)),
            dma((chunks,)),
            dma((chunks,)),
            dma((3, slices, pieces)),
            dma((slices, pieces)),
            dma((3, slices)),
            dma((3, slices)),
        ],
        compiler_params=pltpu.CompilerParams(collective_id=0, has_side_effects=True),
    )(tokens, timestep, padded_heads, by_kind, qkv_weight, out_weight)


def fits(mesh):
    shape = mesh.shape
    return shape["group"] == 2 and shape["blk"] == 2 and shape["tp"] == 2 and shape["seq"] >= 4


def solution(mesh):
    chosen = functools.partial(fused_body, mesh.shape["seq"]) if fits(mesh) else body
    return jax.shard_map(
        chosen,
        mesh=mesh,
        in_specs=(
            P(("group", "blk"), ("seq", "tp")),
            P("group"),
            P("group"),
            P(),
            P(None, "blk", ("seq", "tp")),
            P(("seq", "tp"), "blk"),
        ),
        out_specs=P(("group", "blk"), ("seq", "tp")),
        check_vma=False,
    )
```

```python
import functools
import math

import jax
import jax.numpy as jnp
from jax import lax
from jax.experimental import pallas as pl
from jax.experimental.pallas import tpu as pltpu
from jax.sharding import PartitionSpec as P

epsilon = 1e-06
neg_large = -1e30


def collect(own_part):
    gathered = lax.all_gather(own_part, ("seq", "tp"), axis=1, tiled=True)
    return gathered


def attend_block(running, queries, key_block, value_block, factor):
    largest, totals, weighted = running
    scores = (
        lax.dot_general(
            queries, key_block, (((1,), (1,)), ((), ())), preferred_element_type=jnp.float32
        )
        * factor
    )
    new_max = jnp.maximum(largest, jnp.max(scores, axis=1))
    rescale = jnp.exp(largest - new_max)
    weights = jnp.exp(scores - new_max[:, None])
    totals = totals * rescale + jnp.sum(weights, axis=1)
    weighted = weighted * rescale[:, None] + jnp.dot(
        weights.astype(jnp.bfloat16), value_block, preferred_element_type=jnp.float32
    )
    return (new_max, totals, weighted)


def body(tokens, timestep, padded_heads, modulation, qkv_weight, out_weight):
    slices = lax.axis_size(("seq", "tp"))
    own_index = lax.axis_index(("seq", "tp"))
    model_width = modulation.shape[2]
    own_width = model_width // slices
    token_rows = tokens.shape[0]
    head_size = out_weight.shape[0]
    table_row = lax.dynamic_index_in_dim(modulation, timestep[0], 0, keepdims=False)
    own_entry = lax.dynamic_slice_in_dim(table_row, own_index * own_width, own_width, 1)
    gathered = collect(tokens).astype(jnp.float32)
    average = jnp.mean(gathered, axis=1, keepdims=True)
    centered = gathered - average
    spread = jnp.mean(centered * centered, axis=1, keepdims=True)
    normed = centered * lax.rsqrt(spread + epsilon)
    modulated = (normed * (1.0 + table_row[1]) + table_row[0]).astype(jnp.bfloat16)
    projected = jnp.einsum(
        "td,kde->kte",
        modulated,
        lax.all_gather(qkv_weight, "blk", axis=1, tiled=True),
        preferred_element_type=jnp.float32,
    ).astype(jnp.bfloat16)
    queries = projected[0]
    factor = 1.0 / math.sqrt(head_size)
    initial = (
        jnp.full((token_rows,), neg_large, jnp.float32),
        jnp.zeros((token_rows,), jnp.float32),
        jnp.zeros((token_rows, head_size), jnp.float32),
    )
    key_piece = lax.all_gather(projected[1], "blk", axis=0, tiled=True)
    value_piece = lax.all_gather(projected[2], "blk", axis=0, tiled=True)
    length = key_piece.shape[0]

    def one_block(counter, inner_state):
        key_block = lax.dynamic_slice_in_dim(key_piece, counter * 512, 512, 0)
        value_block = lax.dynamic_slice_in_dim(value_piece, counter * 512, 512, 0)
        return attend_block(inner_state, queries, key_block, value_block, factor)

    largest, exp_totals, weighted = lax.fori_loop(0, length // 512, one_block, initial)
    attended = weighted / exp_totals[:, None]
    live_heads = slices - padded_heads[0]
    masked = jnp.where(own_index < live_heads, attended, 0.0).astype(jnp.bfloat16)
    head_term = jnp.dot(
        masked,
        lax.all_gather(out_weight, "blk", axis=1, tiled=True),
        preferred_element_type=jnp.float32,
    )
    summed = lax.psum_scatter(
        head_term.astype(jnp.bfloat16), ("seq", "tp"), scatter_dimension=1, tiled=True
    ).astype(jnp.float32)
    return (own_entry[2] * summed).astype(jnp.bfloat16)


MESH = pl.DeviceIdType.MESH
bf16, f32 = jnp.bfloat16, jnp.float32


def fused_kernel(
    dims,
    tokens_ref,
    step_ref,
    padded_ref,
    modulation_ref,
    qkv_ref,
    out_weight_ref,
    out_ref,
    step_smem,
    padded_smem,
    modulation,
    tok,
    mod,
    wts,
    query,
    kv,
    att,
    wout,
    outw,
    table,
    lift,
    vectors,
    level,
    sums,
    squares,
    total,
    local_sem,
    tok_send,
    tok_recv,
    w_send,
    w_recv,
    kv_send,
    kv_recv,
    att_send,
    att_recv,
    o_send,
    o_recv,
):
    S, chunks, pieces = dims
    rows, width = tokens_ref.shape
    kinds, half, size = qkv_ref.shape
    slices = 2 * S
    g, z = lax.axis_index("group"), lax.axis_index("seq")
    x, c = lax.axis_index("blk"), lax.axis_index("tp")
    own = z * 2 + c
    R = rows // chunks
    A = rows // pieces
    part = half // 2
    hpart = size // 2

    up, down = (g, z + 1, x, c), (g, z - 1, x, c)
    mate = (g, z, x, 1 - c)
    over = (g, z, 1 - x, c)
    twin = (1 - g, z, x, c)

    def remote(src, dst, s_sem, r_sem, where):
        return pltpu.make_async_remote_copy(
            src_ref=src,
            dst_ref=dst,
            send_sem=s_sem,
            recv_sem=r_sem,
            device_id=where,
            device_id_type=MESH,
        )

    def lanes(index, extent):
        return pl.ds(pl.multiple_of(index * extent, 128), extent)

    def tok_at(s, r):
        return tok.at[pl.ds(r * R, R), lanes(s, width)]

    def att_at(s, r):
        return att.at[pl.ds(r * A, A), lanes(s, size)]

    def tok_copy(way, s, r, where, src=None):
        there = tok_at(s, r)
        return remote(there if src is None else src, there, tok_send.at[way, s, r], tok_recv.at[s, r], where)

    def att_copy(way, s, r, where, src=None):
        there = att_at(s, r)
        return remote(there, there, att_send.at[way, s, r], att_recv.at[s, r], where)

    def send_own(make, r, src=None):
        @pl.when(z < S - 1)
        def _():
            make(0, own, r, up, src).start()

        @pl.when(z > 0)
        def _():
            make(1, own, r, down, src).start()

        make(2, own, r, mate, src).start()

    def relay(make, d, r):
        @pl.when(z - d >= 0)
        def _():
            s = (z - d) * 2 + c
            make(0, s, r, up).wait_recv()

            @pl.when(z < S - 1)
            def _():
                make(0, s, r, up).start()

            make(2, s, r, mate).start()

        @pl.when(z + d < S)
        def _():
            s = (z + d) * 2 + c
            make(1, s, r, down).wait_recv()

            @pl.when(z > 0)
            def _():
                make(1, s, r, down).start()

            make(2, s, r, mate).start()

    def wait_mates(make, r):
        for other in range(S):
            make(2, other * 2 + 1 - c, r, mate).wait_recv()

    def drain(make, count):
        for r in range(count):
            for other in range(S):
                s = other * 2 + c

                @pl.when((z < S - 1) & (other <= z))
                def _():
                    make(0, s, r, up).wait_send()

                @pl.when((z > 0) & (other >= z))
                def _():
                    make(1, s, r, down).wait_send()

                make(2, s, r, mate).wait_send()

    def w_at(block, p, i):
        first = pl.multiple_of(block * half + p * part, 16)
        return wts.at[pl.ds(first, part), pl.ds(i * size, size)]

    def w_over(i):
        src = qkv_ref.at[i, pl.ds(pl.multiple_of(g * part, 16), part)]
        return remote(src, w_at(x, g, i), w_send.at[0, i], w_recv.at[0, i], over)

    def w_over_in(i):
        there = w_at(1 - x, g, i)
        return remote(there, there, w_send.at[0, i], w_recv.at[0, i], over)

    def w_twin(i):
        there = w_at(1 - x, g, i)
        return remote(there, there, w_send.at[1, i], w_recv.at[1, i], twin)

    def w_twin_in(i):
        there = w_at(1 - x, 1 - g, i)
        return remote(there, there, w_send.at[1, i], w_recv.at[1, i], twin)

    def o_at(head, p):
        return wout.at[head, pl.ds(pl.multiple_of(p * hpart, 16), hpart)]

    def o_over(block):
        src = out_weight_ref.at[pl.ds(pl.multiple_of(g * hpart, 16), hpart)]
        return remote(src, outw.at[block], o_send.at[0, 0], o_recv.at[0, 0], over)

    per_blk = slices // 2

    def o_src(s):
        return outw.at[s // per_blk, :, lanes(lax.rem(s, per_blk), width)]

    def o_copy(step):
        s = lax.rem(own + step, slices)
        return remote(o_src(s), o_at(own, g), o_send.at[1, step], o_recv.at[1, own], (g, s // 2, x, s % 2))

    def o_in(head):
        return remote(o_at(head, g), o_at(head, g), o_send.at[1, 0], o_recv.at[1, head], mate)

    def o_twin(head, p):
        return remote(o_at(head, p), o_at(head, p), o_send.at[2, head], o_recv.at[2, head], twin)

    def kv_at(block, r):
        return kv.at[block, :, pl.ds(r * R, R)]

    def kv_copy(block, r):
        return remote(kv_at(block, r), kv_at(block, r), kv_send.at[r], kv_recv.at[r], over)

    barrier = pltpu.get_barrier_semaphore()

    @pl.when(z < S - 1)
    def _():
        pl.semaphore_signal(barrier, inc=1, device_id=up, device_id_type=MESH)

    @pl.when(z > 0)
    def _():
        pl.semaphore_signal(barrier, inc=1, device_id=down, device_id_type=MESH)

    for where in (mate, over, twin):
        pl.semaphore_signal(barrier, inc=1, device_id=where, device_id_type=MESH)
    locals_ = [
        pltpu.make_async_copy(tokens_ref, tok.at[:, lanes(own, width)], local_sem.at[0]),
        pltpu.make_async_copy(step_ref, step_smem, local_sem.at[6]),
        pltpu.make_async_copy(padded_ref, padded_smem, local_sem.at[7]),
        pltpu.make_async_copy(modulation_ref, modulation, local_sem.at[8]),
        pltpu.make_async_copy(
            out_weight_ref.at[pl.ds(pl.multiple_of(g * hpart, 16), hpart)], outw.at[x], local_sem.at[9]
        ),
    ]
    for i in range(kinds):
        there = wts.at[pl.ds(pl.multiple_of(x * half, 16), half), pl.ds(i * size, size)]
        locals_.append(pltpu.make_async_copy(qkv_ref.at[i], there, local_sem.at[1 + i]))
    for copy in locals_:
        copy.start()
    pl.semaphore_wait(barrier, 3 + (z < S - 1).astype(jnp.int32) + (z > 0).astype(jnp.int32))

    for r in range(chunks):
        send_own(tok_copy, r, tokens_ref.at[pl.ds(r * R, R)])
    for i in range(kinds):
        w_over(i).start()
    o_over(x).start()
    for copy in locals_:
        copy.wait()
    row = pl.ds(step_smem[0], 1)
    table[0:1, :] = 1.0 + modulation[1, row, :]
    table[1:2, :] = modulation[0, row, :]
    table[2:3, :] = modulation[2, row, :]

    block = 32
    span = 2 * width
    tile = level.shape[1]

    def fold(values):
        folded = values[:, :tile]
        for i in range(1, values.shape[1] // tile):
            folded = folded + values[:, i * tile : (i + 1) * tile]
        return folded

    def set_level(i, carry):
        at = pl.ds(pl.multiple_of(i * block, block), block)
        values = tok[at, lanes(own, width)].astype(f32)
        level[at, :] = jnp.broadcast_to(jnp.mean(values, axis=1, keepdims=True), (block, tile))
        return carry

    lax.fori_loop(0, rows // block, set_level, 0)
    lift[...] = jnp.zeros_like(lift)
    for i in range(2):
        high = table[i : i + 1, :].astype(bf16).astype(f32)
        lift[2 * i : 2 * i + 1, :] = high
        lift[2 * i + 1 : 2 * i + 2, :] = table[i : i + 1, :] - high

    def set_vectors():
        for i in range(kinds):
            w_twin_in(i).wait_recv()
        product = jnp.dot(lift[...].astype(bf16), wts[...], preferred_element_type=f32)
        vectors[0:1, :] = product[0:1] + product[1:2]
        vectors[1:2, :] = product[2:3] + product[3:4]

    def add_pair(chip, r, count, first=False):
        for i in range(r, r + count):
            tok_copy(2, chip * 2 + 1 - c, i, mate).wait_recv()
        columns = lanes(chip, span)

        def one(i, carry):
            at = pl.ds(pl.multiple_of(r * R + i * block, block), block)
            base = level[at, :]
            shifted = tok[at, columns].astype(f32) - jnp.concatenate([base] * (span // tile), axis=1)
            if first:
                sums[at, :] = fold(shifted)
                squares[at, :] = fold(shifted * shifted)
            else:
                sums[at, :] += fold(shifted)
                squares[at, :] += fold(shifted * shifted)
            mod[pl.ds(pl.multiple_of(i * block, block), block), :] = (shifted * table[0:1, columns]).astype(bf16)
            return carry

        lax.fori_loop(0, count * R // block, one, 0)
        depth = pl.ds(pl.multiple_of(chip * span, 16), span)
        at = pl.ds(r * R, count * R)
        product = jnp.dot(mod[: count * R, :], wts[depth, :], preferred_element_type=f32)
        total[at, :] = product if first else total[at, :] + product

    def add_ring(d, r, count):
        @pl.when(z - d >= 0)
        def _():
            add_pair(z - d, r, count)

        @pl.when(z + d < S)
        def _():
            add_pair(z + d, r, count)

    def finish(r):
        at = pl.ds(r * R, R)
        share = 1.0 / (slices * width)
        offset = jnp.sum(sums[at, :], axis=1, keepdims=True) * share
        spread = jnp.sum(squares[at, :], axis=1, keepdims=True) * share - offset * offset
        rate = lax.rsqrt(jnp.maximum(spread, 0.0) + epsilon)
        projected = ((total[at, :] - offset * vectors[0:1, :]) * rate + vectors[1:2, :]).astype(bf16)
        query[at, :] = projected[:, :size]
        kv[x, 0, at, :] = projected[:, size : 2 * size]
        kv[x, 1, at, :] = projected[:, 2 * size :]
        kv_copy(x, r).start()

    def send_out_weight(inner):
        for step in range(1, slices):
            chip = lax.rem(own + step, slices) // 2

            @pl.when(((chip > 0) & (chip < S - 1)) == inner)
            def _():
                o_copy(step).start()

    forwarded = 0
    for d in range(1, S):
        last = d == S - 1
        for r in range(chunks):
            relay(tok_copy, d, r)
            if r % 2 == 1 and forwarded < kinds:
                w_over_in(forwarded).wait_recv()
                w_twin(forwarded).start()
                forwarded += 1
            if last:
                add_ring(d - 1, r, 1)
                if r > 0:
                    add_ring(d, r - 1, 1)
                    finish(r - 1)
        if d == S - 2:
            set_vectors()
            o_over(1 - x).wait_recv()
            local = pltpu.make_async_copy(o_src(own), o_at(own, g), local_sem.at[5])
            local.start()
            send_out_weight(True)
            for r in range(0, chunks, 2):
                add_pair(z, r, 2, True)
            for near in range(1, d):
                for r in range(0, chunks, 2):
                    add_ring(near, r, 2)

    send_out_weight(False)
    add_ring(S - 1, chunks - 1, 1)
    finish(chunks - 1)
    local.wait()
    o_twin(own, g).start()

    factor = 1.0 / math.sqrt(size)
    contract = (((1,), (1,)), ((), ()))

    live = jnp.full((1, size), padded_smem[0], jnp.int32) < slices - own

    def attend(r):
        q = query[pl.ds(r * A, A), :]
        scores = []
        for b in (x, 1 - x):
            if r == 0 and len(scores) > 0:
                for i in range(chunks):
                    kv_copy(1 - x, i).wait_recv()
            scores.append(lax.dot_general(q, kv[b, 0], contract, preferred_element_type=f32) * factor)
        largest = jnp.maximum(
            jnp.max(scores[0], axis=1, keepdims=True), jnp.max(scores[1], axis=1, keepdims=True)
        )
        total, weighted = 0.0, 0.0
        for b, part_scores in zip((x, 1 - x), scores):
            weights = jnp.exp(part_scores - largest)
            total = total + jnp.sum(weights, axis=1, keepdims=True)
            weighted = weighted + jnp.dot(weights.astype(bf16), kv[b, 1], preferred_element_type=f32)
        attended = weighted / total
        masked = jnp.where(live, attended, 0.0).astype(bf16)
        att[pl.ds(r * A, A), lanes(own, size)] = masked
        send_own(att_copy, r)

    for r in range(pieces):
        attend(r)

    for d in range(1, S):
        for r in range(pieces):
            relay(att_copy, d, r)
        if d == 1:
            for step in range(1, slices):
                head = lax.rem(own + step, slices)
                o_in(head).wait_recv()
                o_twin(head, g).start()

    for head in range(slices):
        o_twin(head, 1 - g).wait_recv()
    gate = table[2:3, lanes(own, width)]
    weight = wout[...].reshape(slices * size, width)
    for r in range(pieces):
        wait_mates(att_copy, r)
        summed = jnp.dot(att[pl.ds(r * A, A), :], weight, preferred_element_type=f32)
        out_ref[pl.ds(r * A, A), :] = (gate * summed).astype(bf16)

    drain(tok_copy, chunks)
    drain(att_copy, pieces)
    for i in range(kinds):
        w_over(i).wait_send()
        w_twin(i).wait_send()
    for r in range(chunks):
        kv_copy(x, r).wait_send()
    o_over(x).wait_send()
    for step in range(1, slices):
        o_copy(step).wait_send()
    for head in range(slices):
        o_twin(head, g).wait_send()


def fused_body(S, tokens, timestep, padded_heads, modulation, qkv_weight, out_weight):
    slices = 2 * S
    rows, width = tokens.shape
    kinds, half, size = qkv_weight.shape
    model_width = modulation.shape[2]
    chunks, pieces = 4, 2
    by_kind = jnp.transpose(modulation, (1, 0, 2))
    anywhere = pl.BlockSpec(memory_space=pltpu.HBM)
    vmem = pl.BlockSpec(memory_space=pltpu.VMEM)
    dma = pltpu.SemaphoreType.DMA
    return pl.pallas_call(
        functools.partial(fused_kernel, (S, chunks, pieces)),
        out_shape=jax.ShapeDtypeStruct((rows, width), bf16),
        in_specs=[anywhere] * 6,
        out_specs=vmem,
        scratch_shapes=[
            pltpu.SMEM((1,), jnp.int32),
            pltpu.SMEM((1,), jnp.int32),
            pltpu.VMEM(by_kind.shape, f32),
            pltpu.VMEM((rows, model_width), bf16),
            pltpu.VMEM((2 * rows // chunks, 2 * width), bf16),
            pltpu.VMEM((model_width, kinds * size), bf16),
            pltpu.VMEM((rows, size), bf16),
            pltpu.VMEM((2, 2, rows, size), bf16),
            pltpu.VMEM((rows, slices * size), bf16),
            pltpu.VMEM((slices, size, width), bf16),
            pltpu.VMEM((2, size // 2, out_weight.shape[1]), bf16),
            pltpu.VMEM((8, model_width), f32),
            pltpu.VMEM((8, model_width), f32),
            pltpu.VMEM((8, kinds * size), f32),
            pltpu.VMEM((rows, 128), f32),
            pltpu.VMEM((rows, 128), f32),
            pltpu.VMEM((rows, 128), f32),
            pltpu.VMEM((rows, kinds * size), f32),
            dma((10,)),
            dma((3, slices, chunks)),
            dma((slices, chunks)),
            dma((2, kinds)),
            dma((2, kinds)),
            dma((chunks,)),
            dma((chunks,)),
            dma((3, slices, pieces)),
            dma((slices, pieces)),
            dma((3, slices)),
            dma((3, slices)),
        ],
        compiler_params=pltpu.CompilerParams(collective_id=0, has_side_effects=True),
    )(tokens, timestep, padded_heads, by_kind, qkv_weight, out_weight)


def fits(mesh):
    shape = mesh.shape
    return shape["group"] == 2 and shape["blk"] == 2 and shape["tp"] == 2 and shape["seq"] >= 4


def solution(mesh):
    chosen = functools.partial(fused_body, mesh.shape["seq"]) if fits(mesh) else body
    return jax.shard_map(
        chosen,
        mesh=mesh,
        in_specs=(
            P(("group", "blk"), ("seq", "tp")),
            P("group"),
            P("group"),
            P(),
            P(None, "blk", ("seq", "tp")),
            P(("seq", "tp"), "blk"),
        ),
        out_specs=P(("group", "blk"), ("seq", "tp")),
        check_vma=False,
    )
```
